256 devices in a mesh: src: 16 (over x, z_lo), rcv: 16 (over z_hi, y, core).
Axes of the slice: x: 4, y: 4, z: 8 (z_hi: 2, z_lo: 4; z = z_hi * 4 + z_lo), core: 2. Of those that a mesh axis runs over, the one named last changes fastest.
Arguments:
- reflection: bfloat16 [2, 8, 16384, 4096], P(None, None, 'src', 'rcv'), may hold values from -0.25 to 0.25
- focusing: bfloat16 [96, 4096, 128], P('src', 'rcv'), may hold values from -6 to 6
- direct: bfloat16 [96, 4096, 128], P('src', 'rcv'), may hold values from -6 to 6
- onset_source: int32 [96, 16384], P(None, 'src'), may hold values from 32 to 128
- onset_receiver: int32 [96, 4096], P('src', 'rcv'), may hold values from 32 to 128
Outputs:
- upgoing: bfloat16 [96, 16384, 128], P('rcv', 'src')
- refocused: float32 [96, 4096, 128], P('src', 'rcv')
The draws below stay inside these ranges and needn't reach their ends.
All inputs are finite; a program needn't handle non-finite values.
Results may differ from the reference program's by a relative error of at most 0.022.
Values may be sent and summed in bfloat16 or wider, within the bound.
No kernel may reach another device: no remote copies, remote signals or barrier semaphores. Data moves between devices by JAX's collectives and lax.ppermute only.
A program may use at most 192 MiB of HBM per device.

```python
import math
import jax
import jax.numpy as jnp
from jax import lax

NS = 16384
NR = 4096
NF = 8
NT = 128
NV = 96
N_SRC = 16
N_RCV = 16


def with_ends(values, key, low, top_value):
    place = [jax.random.randint(jax.random.fold_in(key, axis), (), 0, length) for axis, length in enumerate(values.shape)]
    longest = values.shape.index(max(values.shape))
    beside = place[:longest] + [(place[longest] + 1) % values.shape[longest]] + place[longest + 1:]
    return values.at[tuple(place)].set(low).at[tuple(beside)].set(top_value)


def block_scale(rng, extent, cuts, low, high):
    factor_of = 1.0
    for axis_at, shards_of in cuts:
        draws = jax.random.uniform(jax.random.fold_in(jax.random.fold_in(rng, 6), axis_at), (shards_of,), jnp.float32, low / len(cuts), high / len(cuts))
        factor_of = factor_of * jnp.repeat(jnp.exp(draws), extent[axis_at] // shards_of).reshape((-1,) + (1,) * (len(extent) - 1 - axis_at))
    return factor_of


def bell_draw(stream_key, shape, scale, bound, shards=(), kind=jnp.bfloat16):
    entries = scale * jax.random.normal(stream_key, shape, jnp.float32)
    if shards:
        entries = entries * block_scale(stream_key, shape, shards, -0.22, 0.18)
    return jnp.clip(entries, -bound, bound).astype(kind)


def setup_inputs(seed: int = 0) -> dict:
    arg_keys = jax.random.split(jax.random.key(seed), 6)
    reflection = bell_draw(arg_keys[0], (2, NF, NS, NR), (NR // 9) ** -0.5, 0.25, ((2, 16), (3, 16)))
    focusing = bell_draw(arg_keys[1], (NV, NR, NT), 1.0, 6.0, ((0, 16), (1, 16)))
    direct = bell_draw(arg_keys[2], (NV, NR, NT), 1.0, 6.0, ((0, 16), (1, 16)))
    onset_source = with_ends(jax.random.randint(arg_keys[3], (NV, NS), NT // 4, NT + 1), jax.random.fold_in(arg_keys[3], 1), NT // 4, NT).astype(jnp.int32)
    onset_receiver = with_ends(jax.random.randint(arg_keys[4], (NV, NR), NT // 4, NT + 1), jax.random.fold_in(arg_keys[4], 1), NT // 4, NT).astype(jnp.int32)
    return dict(reflection=reflection, focusing=focusing, direct=direct, onset_source=onset_source, onset_receiver=onset_receiver)


def tables():
    steps_t = jnp.arange(NT, dtype=jnp.int32)
    bins = jnp.arange(1, NF + 1, dtype=jnp.int32)
    phase = (2.0 * math.pi / NT) * ((bins[:, None] * steps_t[None, :]) % NT).astype(jnp.float32)
    return jnp.cos(phase), jnp.sin(phase)


def to_spectra(field, cosines, sines):
    real_part = jnp.einsum("kt,vxt->kxv", cosines, field, precision=lax.Precision.HIGHEST)
    imaginary_component = -jnp.einsum("kt,vxt->kxv", sines, field, precision=lax.Precision.HIGHEST)
    return real_part, imaginary_component


def to_samples(real_part, imaginary_component, cosines, sines):
    first = jnp.einsum("kxv,kt->vxt", real_part, cosines, precision=lax.Precision.HIGHEST)
    second = jnp.einsum("kxv,kt->vxt", imaginary_component, sines, precision=lax.Precision.HIGHEST)
    return (2.0 / NT) * (first - second)


def time_window(field, onsets):
    steps_t = jnp.arange(NT, dtype=jnp.int32)
    keep = steps_t[None, None, :] < onsets[:, :, None]
    return jnp.where(keep, field, jnp.zeros_like(field))


def block_total(partials):
    rounded_values = lax.optimization_barrier(partials.astype(jnp.bfloat16))
    return jnp.sum(rounded_values.astype(jnp.float32), axis=0)


def reference(reflection, focusing, direct, onset_source, onset_receiver):
    cosines, sines = tables()
    fre, fim = to_spectra(focusing.astype(jnp.float32), cosines, sines)
    fre = fre.astype(jnp.bfloat16)
    fim = fim.astype(jnp.bfloat16)
    width_r = NR // N_RCV
    width_s = NS // N_SRC

    def convolve(items):
        rre, rim, sre, sim = items
        left_re = rre.astype(jnp.float32).reshape(NS, N_RCV, width_r)
        left_im = rim.astype(jnp.float32).reshape(NS, N_RCV, width_r)
        right_re = sre.astype(jnp.float32).reshape(N_RCV, width_r, NV)
        right_im = sim.astype(jnp.float32).reshape(N_RCV, width_r, NV)
        real_component = jnp.einsum("sjr,jrv->jsv", left_re, right_re) - jnp.einsum("sjr,jrv->jsv", left_im, right_im)
        part_im = jnp.einsum("sjr,jrv->jsv", left_re, right_im) + jnp.einsum("sjr,jrv->jsv", left_im, right_re)
        return block_total(real_component), block_total(part_im)

    ure, uim = lax.map(convolve, (reflection[0], reflection[1], fre, fim))
    upgoing = time_window(to_samples(ure, uim, cosines, sines), onset_source).astype(jnp.bfloat16)
    wre, wim = to_spectra(upgoing.astype(jnp.float32), cosines, sines)
    wre = wre.astype(jnp.bfloat16)
    wim = wim.astype(jnp.bfloat16)

    def correlate(items):
        rre, rim, are, aim = items
        left_re = rre.astype(jnp.float32).reshape(N_SRC, width_s, NR)
        left_im = rim.astype(jnp.float32).reshape(N_SRC, width_s, NR)
        right_re = are.astype(jnp.float32).reshape(N_SRC, width_s, NV)
        right_im = aim.astype(jnp.float32).reshape(N_SRC, width_s, NV)
        real_component = jnp.einsum("jsr,jsv->jrv", left_re, right_re) + jnp.einsum("jsr,jsv->jrv", left_im, right_im)
        part_im = jnp.einsum("jsr,jsv->jrv", left_re, right_im) - jnp.einsum("jsr,jsv->jrv", left_im, right_re)
        return block_total(real_component), block_total(part_im)

    gre, gim = lax.map(correlate, (reflection[0], reflection[1], wre, wim))
    downward = to_samples(gre, gim, cosines, sines)
    refocused = direct.astype(jnp.float32) + time_window(downward, onset_receiver)
    return upgoing, refocused
```

```python
import functools
import math

import jax
import jax.numpy as jnp
import numpy as np
from jax import lax
from jax.experimental import pallas as pl
from jax.experimental.pallas import tpu as pltpu
from jax.sharding import PartitionSpec as P

NF = 8
NT = 128
NP = 6
ROWS = 2 * NF * NP
NS = 1024
NR = 256
BF = jnp.bfloat16
F32 = jnp.float32
WINDOWS = ((0, 16), (0, 32), (16, 32), (32, 16))


def split(table):
    high = table.astype(BF)
    low = (table - high.astype(np.float32)).astype(BF)
    return high, low


def tables():
    k = np.arange(1, NF + 1)[:, None]
    t = np.arange(NT)[None, :]
    phase = 2.0 * math.pi / NT * ((k * t) % NT)
    return np.cos(phase).astype(np.float32), np.sin(phase).astype(np.float32)


def spectra_table():
    cosines, sines = tables()
    full = np.zeros((NP, NF, NP, 2, NT), np.float32)
    for j in range(NP):
        full[j, :, j, 0] = cosines
        full[j, :, j, 1] = -sines
    return np.concatenate(split(full.reshape(NP, ROWS, NT)), axis=1)


def samples_table():
    cosines, sines = tables()
    full = np.zeros((NP, NT, NF, NP, 2), np.float32)
    for j in range(NP):
        full[j, :, :, j, 0] = 2.0 / NT * cosines.T
        full[j, :, :, j, 1] = -2.0 / NT * sines.T
    high, low = split(full.reshape(NP, NT, ROWS))
    return np.concatenate([high, high, low], axis=2)


def dot(a, b, ca=1, cb=0):
    return lax.dot_general(a, b, (((ca,), (cb,)), ((), ())), preferred_element_type=F32)


def hi_lo_hi(x, axis):
    high = x.astype(BF)
    low = (x - high.astype(F32)).astype(BF)
    return jnp.concatenate([high, low, high], axis=axis)


def place():
    src = lax.axis_index("src")
    rcv = lax.axis_index("rcv")
    return src // 4, src % 4, rcv // 8, (rcv // 2) % 4, rcv % 2


def call(kernel, out, name, **kw):
    params = kw.pop("params", {})
    return pl.pallas_call(
        kernel,
        out_shape=out,
        name=name,
        compiler_params=pltpu.CompilerParams(vmem_limit_bytes=48 << 20, **params),
        **kw,
    )


def spectra_kernel(f_ref, t_ref, o_ref):
    acc = jnp.zeros((2 * ROWS, NR), F32)
    for j in range(NP):
        acc += dot(t_ref[j], f_ref[j], 1, 1)
    o_ref[...] = (acc[:ROWS] + acc[ROWS:]).astype(BF)


def swap_rows(x):
    even = lax.broadcasted_iota(jnp.int32, x.shape, 0) % 2 == 0
    n = x.shape[0]
    return jnp.where(even, -pltpu.roll(x, n - 1, 0), pltpu.roll(x, 1, 0))


def conv_kernel(other, f0, f1, f2, f3, r_ref, o_ref, l1, l2):
    @pl.when((pl.program_id(0) == 0) & (pl.program_id(1) == 0))
    def _():
        x, zl, zh, y, c = place()
        core = lax.rem(c + other, 2)
        par = lax.rem(zl + core, 2)
        for dx, ref in enumerate((f0, f1, f2, f3)):
            for h in range(2):
                dz = 2 * h + par
                xb = lax.rem(x + 4 - dx, 4)
                zb = lax.rem(zl + 4 - dz, 4)
                zhb = xb // 2
                yb = lax.rem(xb, 2) * 2 + zb // 2
                to = lax.rem(yb + 4 - y, 4) * 2 + lax.rem(zhb + zh, 2)
                rows = ref[dz].astype(F32)
                swapped = swap_rows(rows)
                for k in range(NF):
                    lo = 24 * (k // 2) + 8 * (k % 2)
                    l1[k, to] = rows[lo : lo + 16].astype(BF)
                    l2[k, to] = swapped[lo : lo + 16].astype(BF)

    pair = pl.program_id(0)
    u = []
    for i in range(2):
        k = 2 * pair + i
        a1 = l1[k].reshape(128, NR)
        a2 = l2[k].reshape(128, NR)
        v = dot(a1, r_ref[0, i], 1, 1) + dot(a2, r_ref[1, i], 1, 1)
        u.append(v.reshape(8, 16, v.shape[-1]))
    first = lax.broadcasted_iota(jnp.int32, (8, 8, u[0].shape[-1]), 1) < 4
    mixed = jnp.where(first, u[0][:, 8:16], u[1][:, 0:8])
    o_ref[:, 0] = jnp.concatenate([u[0][:, 0:8], mixed, u[1][:, 8:16]], axis=1).astype(BF)


def convolve(pieces, reflection, other):
    sb = 512
    out = call(
        functools.partial(conv_kernel, other),
        jax.ShapeDtypeStruct((8, 4, 24, NS), BF),
        "conv_send" if other else "conv_keep",
        grid=(4, NS // sb),
        in_specs=[pl.BlockSpec((4, ROWS, NR), lambda p, s: (0, 0, 0))] * 4
        + [pl.BlockSpec((2, 2, sb, NR), lambda p, s: (0, p, s, 0))],
        out_specs=pl.BlockSpec((8, 1, 24, sb), lambda p, s: (0, p, 0, s)),
        scratch_shapes=[pltpu.VMEM((NF, 8, 16, NR), BF)] * 2,
        cost_estimate=pl.CostEstimate(flops=1 << 30, bytes_accessed=10 << 20, transcendentals=0),
    )(*pieces, reflection)
    return out.reshape(4, 2, ROWS, NS)


def window_kernel(k_ref, r_ref, on_ref, a_ref, t_ref, w_ref, up_ref):
    u = hi_lo_hi(k_ref[...] + r_ref[...].astype(F32), 0)
    steps = lax.broadcasted_iota(jnp.int32, (NT, NS), 0)
    acc = jnp.zeros((2 * ROWS, NS), F32)
    for j in range(NP):
        field = dot(a_ref[j], u)
        field = jnp.where(steps < on_ref[j : j + 1, :], field, 0.0).astype(BF)
        up_ref[j] = field
        acc += dot(t_ref[j], field)
    w_ref[...] = (acc[:ROWS] + acc[ROWS:]).astype(BF)


def corr_kernel(other, w0, w1, w2, w3, r_ref, o_ref, acc):
    s = pl.program_id(1)

    @pl.when(s == 0)
    def _():
        acc[...] = jnp.zeros_like(acc)

    at = 0
    for i, (lo, n) in enumerate(WINDOWS):
        m = jnp.concatenate([w[e, 0, lo : lo + n] for w in (w0, w1, w2, w3) for e in range(2)], axis=0)
        for part in range(2):
            acc[part, at : at + 8 * n] += dot(m, r_ref[part, i])
        at += 8 * n

    @pl.when(s == pl.num_programs(1) - 1)
    def _():
        x, zl, zh, y, c = place()
        even = lax.broadcasted_iota(jnp.int32, (768, NR), 0) % 2 == 0
        q = acc[1]
        g = acc[0] + jnp.where(even, pltpu.roll(q, 767, 0), -pltpu.roll(q, 1, 0))
        first = lax.broadcasted_iota(jnp.int32, (8, NR), 0) < 4
        for d in range(4):
            yb = lax.rem(y + 4 - d, 4)
            for e in range(2):
                zhb = lax.rem(zh + e, 2)
                xb = zhb * 2 + yb // 2
                b = 2 * d + e
                g0 = g[16 * b : 16 * b + 16]
                g1 = g[128 + 32 * b : 128 + 32 * b + 32]
                g2 = g[384 + 32 * b : 384 + 32 * b + 32]
                g3 = g[640 + 16 * b : 640 + 16 * b + 16]
                rows = jnp.concatenate(
                    [
                        g0[0:8],
                        jnp.where(first, g0[8:16], g1[8:16]),
                        g1[16:24],
                        g2[8:16],
                        jnp.where(first, g2[16:24], g3[0:8]),
                        g3[8:16],
                    ],
                    axis=0,
                )
                o_ref[lax.rem(xb + 4 - x, 4), lax.rem(yb, 2), 0] = rows.astype(BF)


def correlate(waves, reflection, other):
    sb = 512
    return call(
        functools.partial(corr_kernel, other),
        jax.ShapeDtypeStruct((4, 2, 2, 48, NR), BF),
        "corr_other" if other else "corr_own",
        grid=(2, NS // sb),
        in_specs=[pl.BlockSpec((2, 1, 48, sb), lambda q, s: (0, q, 0, s))] * 4
        + [pl.BlockSpec((2, 4, sb, NR), lambda q, s: (0, q, s, 0))],
        out_specs=pl.BlockSpec((4, 2, 1, 48, NR), lambda q, s: (0, 0, q, 0, 0)),
        scratch_shapes=[pltpu.VMEM((2, 768, NR), F32)],
        cost_estimate=pl.CostEstimate(flops=1 << 30, bytes_accessed=10 << 20, transcendentals=0),
    )(*[w.reshape(2, 2, 48, NS) for w in waves], reflection).reshape(4, 2, ROWS, NR)


def refocus_kernel(g0, g1, g2, g3, d_ref, on_ref, a_ref, o_ref):
    g = (g0[...].astype(F32) + g1[...].astype(F32)) + (g2[...].astype(F32) + g3[...].astype(F32))
    gt = hi_lo_hi(g.T, 1)
    steps = lax.broadcasted_iota(jnp.int32, (NR, NT), 1)
    for j in range(NP):
        field = dot(gt, a_ref[j], 1, 1)
        field = jnp.where(steps < on_ref[:, j : j + 1], field, 0.0)
        o_ref[j] = d_ref[j].astype(F32) + field


def send(value, axis, to):
    return lax.ppermute(value, axis, [(i, to(i)) for i in range(16)])


def to_x(d):
    return lambda i: (i // 4 + d) % 4 * 4 + i % 4


def to_zl(d):
    return lambda i: i // 4 * 4 + (i % 4 + d) % 4


def to_y(d):
    return lambda i: i // 8 * 8 + (i // 2 % 4 + d) % 4 * 2 + i % 2


def to_zh(i):
    return (i + 8) % 16


def to_core(i):
    return i ^ 1


def on_device(reflection, focusing, direct, onset_source, onset_receiver):
    x, zl, zh, y, c = place()
    t_spec = jnp.asarray(spectra_table())
    t_samp = jnp.asarray(samples_table())
    vm = pl.BlockSpec(memory_space=pltpu.VMEM)

    spectra = call(spectra_kernel, jax.ShapeDtypeStruct((ROWS, NR), BF), "spectra")(focusing, t_spec)
    stack = jnp.stack([spectra] + [send(spectra, "src", to_zl(d)) for d in (1, 2, 3)])
    pieces = [stack] + [send(stack, "src", to_x(d)) for d in (1, 2, 3)]

    onsets = lax.dynamic_slice_in_dim(onset_source, lax.axis_index("rcv") * NP, NP, 0)
    give = convolve(pieces, reflection, 1)
    got = send(give, "rcv", to_core)
    keep = convolve(pieces, reflection, 0)
    both = [(keep[d].astype(F32) + got[d].astype(F32)).astype(BF) for d in range(4)]
    for d in (1, 2, 3):
        both[d] = send(both[d], "rcv", to_y(d))
    total = (both[0].astype(F32) + both[1].astype(F32)) + (both[2].astype(F32) + both[3].astype(F32))
    half = send(total[1].astype(BF), "rcv", to_zh)
    wave, field = call(
        window_kernel,
        (jax.ShapeDtypeStruct((ROWS, NS), BF), jax.ShapeDtypeStruct((NP, NT, NS), BF)),
        "window",
    )(total[0], half, onsets, t_samp, t_spec)
    upgoing = field.transpose(0, 2, 1)

    pair = jnp.stack([wave, send(wave, "rcv", to_zh)])
    own = [pair] + [send(pair, "rcv", to_y(d)) for d in (1, 2, 3)]
    others = [send(w, "rcv", to_core) for w in own]
    g_own = correlate(own, reflection, 0)
    g_other = correlate(others, reflection, 1)
    halves = [jnp.where(c == 0, g_own, g_other), jnp.where(c == 0, g_other, g_own)]
    back = jnp.stack(halves, axis=2).reshape(4, 4, ROWS, NR)
    parts = [back[0]] + [send(back[d], "src", to_x(d)) for d in (1, 2, 3)]
    summed = ((parts[0].astype(F32) + parts[1].astype(F32)) + (parts[2].astype(F32) + parts[3].astype(F32))).astype(BF)
    last = [
        lax.dynamic_index_in_dim(summed, (zl + d) % 4, 0, keepdims=False) for d in range(4)
    ]
    last = [last[0]] + [send(last[d], "src", to_zl(d)) for d in (1, 2, 3)]
    refocused = call(refocus_kernel, jax.ShapeDtypeStruct((NP, NR, NT), F32), "refocus")(
        *last, direct, onset_receiver.T, t_samp
    )
    return (upgoing, refocused)


def solution(mesh):
    in_specs = (
        P(None, None, "src", "rcv"),
        P("src", "rcv", None),
        P("src", "rcv", None),
        P(None, "src"),
        P("src", "rcv"),
    )
    out_specs = (P("rcv", "src", None), P("src", "rcv", None))
    return jax.shard_map(
        on_device, mesh=mesh, in_specs=in_specs, out_specs=out_specs, check_vma=False
    )
```

```python
import functools
import math

import jax
import jax.numpy as jnp
import numpy as np
from jax import lax
from jax.experimental import pallas as pl
from jax.experimental.pallas import tpu as pltpu
from jax.sharding import PartitionSpec as P

NF = 8
NT = 128
NP = 6
PC = 3
CH = NP // PC
ROWS = 2 * NF * PC
BIN = 2 * PC
NS = 1024
NR = 256
BF = jnp.bfloat16
F32 = jnp.float32


def split(table):
    high = table.astype(BF)
    low = (table - high.astype(np.float32)).astype(BF)
    return high, low


def tables():
    k = np.arange(1, NF + 1)[:, None]
    t = np.arange(NT)[None, :]
    phase = 2.0 * math.pi / NT * ((k * t) % NT)
    return np.cos(phase).astype(np.float32), np.sin(phase).astype(np.float32)


def trace_table():
    cosines, sines = tables()
    return np.concatenate(split(np.stack([cosines, -sines], 1).reshape(2 * NF, NT)))


def order_table():
    move = np.zeros((CH, NF, PC, 2, NP, NF, 2), np.float32)
    for j in range(NP):
        for k in range(NF):
            for part in range(2):
                move[j // PC, k, j % PC, part, j, k, part] = 1
    return move.reshape(CH * ROWS, NP * 2 * NF).astype(BF)


def spectra_table():
    cosines, sines = tables()
    full = np.zeros((PC, NF, PC, 2, NT), np.float32)
    for j in range(PC):
        full[j, :, j, 0] = cosines
        full[j, :, j, 1] = -sines
    return np.concatenate(split(full.reshape(PC, ROWS, NT)), axis=1)


def samples_table():
    cosines, sines = tables()
    full = np.zeros((PC, NT, NF, PC, 2), np.float32)
    for j in range(PC):
        full[j, :, :, j, 0] = 2.0 / NT * cosines.T
        full[j, :, :, j, 1] = -2.0 / NT * sines.T
    high, low = split(full.reshape(PC, NT, ROWS))
    return np.concatenate([high, high, low], axis=2)


def dot(a, b, ca=1, cb=0):
    return lax.dot_general(a, b, (((ca,), (cb,)), ((), ())), preferred_element_type=F32)


def hi_lo_hi(x, axis):
    high = x.astype(BF)
    low = (x - high.astype(F32)).astype(BF)
    return jnp.concatenate([high, low, high], axis=axis)


def place():
    src = lax.axis_index("src")
    rcv = lax.axis_index("rcv")
    return src // 4, src % 4, rcv // 8, (rcv // 2) % 4, rcv % 2


def call(kernel, out, name, mib=8, **kw):
    return pl.pallas_call(
        kernel,
        out_shape=out,
        name=name,
        compiler_params=pltpu.CompilerParams(vmem_limit_bytes=mib << 20),
        **kw,
    )


def cost(us):
    return pl.CostEstimate(flops=int(us * 1e9), bytes_accessed=1 << 16, transcendentals=0)


def window_of(k, tile):
    low = BIN * k // tile * tile
    high = -(-BIN * (k + 1) // tile) * tile
    return low, high


def merge(parts, t, tile):
    bins = sorted({(8 * t) // BIN, (8 * t + 7) // BIN})
    out = None
    for k in bins:
        value = parts[k][..., 8 * t - window_of(k, tile)[0] :, :][..., :8, :]
        if out is None:
            out = value
        else:
            row = lax.broadcasted_iota(jnp.int32, value.shape, value.ndim - 2) + 8 * t
            out = jnp.where(row < BIN * k, out, value)
    return out


def spectra_kernel(f_ref, t_ref, m_ref, o_ref):
    rows = []
    for j in range(NP):
        both = dot(t_ref[...], f_ref[j], 1, 1)
        rows.append(both[: 2 * NF] + both[2 * NF :])
    o_ref[...] = dot(m_ref[...], jnp.concatenate(rows, axis=0).astype(BF)).astype(BF)


def swap_rows(x):
    even = lax.broadcasted_iota(jnp.int32, x.shape, 0) % 2 == 0
    n = x.shape[0]
    return jnp.where(even, -pltpu.roll(x, n - 1, 0), pltpu.roll(x, 1, 0))


def conv_kernel(f0, f1, f2, f3, r_ref, give, keep, l1, l2):
    x, zl, zh, y, c = place()
    for dx, ref in enumerate((f0, f1, f2, f3)):
        for dz in range(4):
            xb = lax.rem(x + 4 - dx, 4)
            zb = zl ^ dz
            yb = lax.rem(xb, 2) * 2 + zb // 2
            to = lax.rem(zb + c, 2) * 8 + lax.rem(yb + 4 - y, 4) * 2 + lax.rem(xb // 2 + zh, 2)
            rows = ref[dz].astype(F32)
            l1[to] = rows
            l2[to] = swap_rows(rows)

    sb = 256

    def step(i, carry):
        g, at = i // 4, pl.ds(pl.multiple_of(lax.rem(i, 4) * sb, sb), sb)
        parts = {}
        for k in range(4):
            low, high = window_of(k, 8)
            n = 16 * (high - low)
            rows = pl.ds(pl.multiple_of(g * 24, 8) + low, high - low)
            a1 = l1[:, rows].reshape(n, NR).astype(BF)
            a2 = l2[:, rows].reshape(n, NR).astype(BF)
            v = dot(a1, r_ref[0, 4 * g + k, at, :], 1, 1) + dot(a2, r_ref[1, 4 * g + k, at, :], 1, 1)
            parts[k] = v.reshape(16, high - low, sb)
        out = jnp.concatenate([merge(parts, t, 8) for t in range(3)], axis=1).astype(BF)
        keep[:, g, :, at] = out[:8]
        give[:, g, :, at] = out[8:]
        return carry

    lax.fori_loop(0, 2 * NS // sb, step, 0)


def convolve(pieces, reflection):
    give, keep = call(
        conv_kernel,
        [jax.ShapeDtypeStruct((8, 2, ROWS // 2, NS), BF)] * 2,
        "conv",
        in_specs=[pl.BlockSpec(memory_space=pltpu.VMEM)] * 5,
        scratch_shapes=[pltpu.VMEM((16, ROWS, NR), F32)] * 2,
        cost_estimate=cost(4),
    )(*pieces, reflection)
    return give.reshape(4, 2, ROWS, NS), keep.reshape(4, 2, ROWS, NS)


def window_kernel(p0, p1, p2, p3, r_ref, on_ref, a_ref, t_ref, w_ref, up_ref):
    steps = lax.broadcasted_iota(jnp.int32, (NT, NS), 0)
    for e in range(2):
        total = (p0[e].astype(F32) + p1[e].astype(F32)) + (p2[e].astype(F32) + p3[e].astype(F32))
        u = hi_lo_hi(total + r_ref[1 - e].astype(F32), 0)
        acc = jnp.zeros((2 * ROWS, NS), F32)
        for j in range(PC):
            field = dot(a_ref[j], u)
            at = e * PC + j
            field = jnp.where(steps < on_ref[at : at + 1, :], field, 0.0).astype(BF)
            if e == 0:
                up_ref[j] = field
            acc += dot(t_ref[j], field)
        w_ref[e] = (acc[:ROWS] + acc[ROWS:]).astype(BF)


def flip_kernel(a_ref, b_ref, o_ref):
    for i, ref in enumerate((a_ref, b_ref)):
        for j in range(PC):
            o_ref[i * PC + j] = ref[j].T


def load_kernel(r_hbm, o_ref, sem):
    copies = [
        pltpu.make_async_copy(r_hbm.at[part, k], o_ref.at[part, k], sem.at[part, k])
        for k in range(NF)
        for part in range(2)
    ]
    for copy in copies:
        copy.start()
    for copy in copies:
        copy.wait()


def corr_kernel(w0, w1, w2, w3, v0, v1, v2, v3, r_ref, o0, o1, o2, o3, out):
    x, zl, zh, y, c = place()
    refs = (w0, w1, w2, w3, v0, v1, v2, v3)
    parts = {}
    for k in range(NF):
        low, high = window_of(k, 16)
        m = jnp.concatenate([w[e, low:high] for w in refs for e in range(2)], axis=0)
        n = m.shape[0]
        q = dot(m, r_ref[1, k])
        even = lax.broadcasted_iota(jnp.int32, q.shape, 0) % 2 == 0
        g = dot(m, r_ref[0, k]) + jnp.where(even, pltpu.roll(q, n - 1, 0), -pltpu.roll(q, 1, 0))
        parts[k] = g.reshape(16, high - low, NR)
    rows = jnp.concatenate([merge(parts, t, 16) for t in range(ROWS // 8)], axis=1).astype(BF)
    for i in range(16):
        other, d, e = i // 8, i // 2 % 4, i % 2
        yb = lax.rem(y + 4 - d, 4)
        xb = lax.rem(zh + e, 2) * 2 + yb // 2
        zb = lax.rem(yb, 2) * 2 + lax.rem(c + other, 2)
        out[lax.rem(xb + 4 - x, 4), zb ^ zl] = rows[i]
    for d, ref in enumerate((o0, o1, o2, o3)):
        ref[...] = out[d]


def correlate(waves, reflection):
    return call(
        corr_kernel,
        [jax.ShapeDtypeStruct((4, ROWS, NR), BF)] * 4,
        "corr",
        in_specs=[pl.BlockSpec(memory_space=pltpu.VMEM)] * 9,
        scratch_shapes=[pltpu.VMEM((4, 4, ROWS, NR), BF)],
        cost_estimate=cost(4),
        mib=16,
    )(*waves, reflection)


def sum_kernel(*refs):
    ins, (keep, *gives) = refs[: 4 * CH], refs[4 * CH :]
    for h in range(CH):
        g = ins[4 * h : 4 * h + 4]
        total = (g[0][...].astype(F32) + g[1][...].astype(F32)) + (g[2][...].astype(F32) + g[3][...].astype(F32))
        keep[h] = total[0]
        for d, give in enumerate(gives):
            give[h] = total[d + 1].astype(BF)


def refocus_kernel(g0, g1, g2, g3, d_ref, on_ref, a_ref, o_ref):
    steps = lax.broadcasted_iota(jnp.int32, (NR, NT), 1)
    for h in range(CH):
        g = (g0[h] + g1[h].astype(F32)) + (g2[h].astype(F32) + g3[h].astype(F32))
        gt = hi_lo_hi(g.T, 1)
        for i in range(PC):
            j = h * PC + i
            field = dot(gt, a_ref[i], 1, 1)
            field = jnp.where(steps < on_ref[:, j : j + 1], field, 0.0)
            o_ref[j] = d_ref[j].astype(F32) + field


def send(value, axis, to):
    return lax.ppermute(value, axis, [(i, to(i)) for i in range(16)])


def to_x(d):
    return lambda i: (i // 4 + d) % 4 * 4 + i % 4


def to_zl(d):
    return lambda i: i ^ d


def to_y(d):
    return lambda i: i // 8 * 8 + (i // 2 % 4 + d) % 4 * 2 + i % 2


def to_zh(i):
    return (i + 8) % 16


def to_core(i):
    return i ^ 1


def after(value, *others):
    return lax.optimization_barrier((value, *others))[0]


def on_device(reflection, focusing, direct, onset_source, onset_receiver):
    t_spec = jnp.asarray(spectra_table())
    t_samp = jnp.asarray(samples_table())

    spectra = call(spectra_kernel, jax.ShapeDtypeStruct((CH * ROWS, NR), BF), "spectra")(
        focusing, jnp.asarray(trace_table()), jnp.asarray(order_table())
    )
    rcv = lax.axis_index("rcv")
    near_far = [lax.dynamic_slice_in_dim(onset_source, r * NP, NP, 0) for r in (rcv, rcv ^ 8)]
    onsets = [jnp.concatenate([o[h * PC : (h + 1) * PC] for o in near_far]) for h in range(CH)]
    near = [spectra] + [send(spectra, "src", to_zl(d)) for d in (1, 2, 3)]
    stacks = [jnp.stack([n[h * ROWS : (h + 1) * ROWS] for n in near]) for h in range(CH)]
    pieces = [[stacks[0]] + [send(stacks[0], "src", to_x(d)) for d in (1, 2, 3)]]
    held = call(
        load_kernel,
        pltpu.VMEM((2, NF, NS, NR), BF),
        "load",
        in_specs=[pl.BlockSpec(memory_space=pltpu.HBM)],
        out_specs=pl.BlockSpec(memory_space=pltpu.VMEM),
        scratch_shapes=[pltpu.SemaphoreType.DMA((2, NF))],
        cost_estimate=cost(3),
        mib=50,
    )(after(reflection, stacks[0]))

    def summed(give, keep):
        got = send(give, "rcv", to_core)
        return [(keep[d].astype(F32) + got[d].astype(F32)).astype(BF) for d in range(4)]

    def over_y(both):
        return [both[0]] + [send(both[d], "rcv", to_y(d)) for d in (1, 2, 3)]

    def half_sum(both):
        return ((both[0].astype(F32) + both[1].astype(F32)) + (both[2].astype(F32) + both[3].astype(F32))).astype(BF)

    def window(both, half, h):
        return call(
            window_kernel,
            (jax.ShapeDtypeStruct((2, ROWS, NS), BF), jax.ShapeDtypeStruct((PC, NT, NS), BF)),
            "window",
            cost_estimate=cost(2),
        )(*both, half, onsets[h], t_samp, t_spec)

    give_a, keep_a = convolve(pieces[0], held)
    second = after(stacks[1], keep_a)
    pieces.append([second] + [send(second, "src", to_x(d)) for d in (1, 2, 3)])
    sum_a = summed(give_a, keep_a)
    sum_b = summed(*convolve(pieces[1], held))
    both_a = over_y(sum_a)
    sum_b[1:] = lax.optimization_barrier((*sum_b[1:], both_a[3]))[:3]
    both_b = over_y(sum_b)
    half_a = send(half_sum(both_a), "rcv", to_zh)
    half_a, part_b = lax.optimization_barrier((half_a, half_sum(both_b)))
    half_b = send(part_b, "rcv", to_zh)
    wave_a, field_a = window(both_a, half_a, 0)
    wave_b, field_b = window(both_b, half_b, 1)
    own_a = over_y([wave_a] * 4)
    own_b = over_y([wave_b] * 4)
    upgoing = call(
        flip_kernel, jax.ShapeDtypeStruct((NP, NS, NT), BF), "flip", cost_estimate=cost(2)
    )(field_a, field_b)
    parts = []
    own_a[0] = after(own_a[0], upgoing)
    for own in (own_a, own_b):
        others = [send(w, "rcv", to_core) for w in own]
        back = correlate([*own, *others], held)
        parts += [back[0]] + [send(back[d], "src", to_x(d)) for d in (1, 2, 3)]

    keep, *gives = call(
        sum_kernel,
        [jax.ShapeDtypeStruct((CH, ROWS, NR), F32)] + [jax.ShapeDtypeStruct((CH, ROWS, NR), BF)] * 3,
        "sum_x",
    )(*parts)
    last = [keep] + [send(gives[d - 1], "src", to_zl(d)) for d in (1, 2, 3)]
    refocused = call(refocus_kernel, jax.ShapeDtypeStruct((NP, NR, NT), F32), "refocus")(
        *last, direct, onset_receiver.T, t_samp
    )
    return (upgoing, refocused)


def solution(mesh):
    in_specs = (
        P(None, None, "src", "rcv"),
        P("src", "rcv", None),
        P("src", "rcv", None),
        P(None, "src"),
        P("src", "rcv"),
    )
    out_specs = (P("rcv", "src", None), P("src", "rcv", None))
    return jax.shard_map(
        on_device, mesh=mesh, in_specs=in_specs, out_specs=out_specs, check_vma=False
    )
```

```python
import functools
import math

import jax
import jax.numpy as jnp
import numpy as np
from jax import lax
from jax.experimental import pallas as pl
from jax.experimental.pallas import tpu as pltpu
from jax.sharding import PartitionSpec as P

NF = 8
NT = 128
NP = 6
PC = 3
CH = NP // PC
ROWS = 2 * NF * PC
BIN = 2 * PC
NS = 1024
NR = 256
BF = jnp.bfloat16
F32 = jnp.float32


def split(table):
    high = table.astype(BF)
    low = (table - high.astype(np.float32)).astype(BF)
    return high, low


def tables():
    k = np.arange(1, NF + 1)[:, None]
    t = np.arange(NT)[None, :]
    phase = 2.0 * math.pi / NT * ((k * t) % NT)
    return np.cos(phase).astype(np.float32), np.sin(phase).astype(np.float32)


def trace_table():
    cosines, sines = tables()
    return np.concatenate(split(np.stack([cosines, -sines], 1).reshape(2 * NF, NT)))


def spectra_table():
    cosines, sines = tables()
    full = np.zeros((PC, NF, PC, 2, NT), np.float32)
    for j in range(PC):
        full[j, :, j, 0] = cosines
        full[j, :, j, 1] = -sines
    return np.concatenate(split(full.reshape(PC, ROWS, NT)), axis=1)


def samples_table():
    cosines, sines = tables()
    full = np.zeros((PC, NT, NF, PC, 2), np.float32)
    for j in range(PC):
        full[j, :, :, j, 0] = 2.0 / NT * cosines.T
        full[j, :, :, j, 1] = -2.0 / NT * sines.T
    high, low = split(full.reshape(PC, NT, ROWS))
    return np.concatenate([high, high, low], axis=2)


def dot(a, b, ca=1, cb=0):
    return lax.dot_general(a, b, (((ca,), (cb,)), ((), ())), preferred_element_type=F32)


def hi_lo_hi(x, axis):
    high = x.astype(BF)
    low = (x - high.astype(F32)).astype(BF)
    return jnp.concatenate([high, low, high], axis=axis)


def place():
    src = lax.axis_index("src")
    rcv = lax.axis_index("rcv")
    return src // 4, src % 4, rcv // 8, (rcv // 2) % 4, rcv % 2


def call(kernel, out, name, mib=8, **kw):
    return pl.pallas_call(
        kernel,
        out_shape=out,
        name=name,
        compiler_params=pltpu.CompilerParams(vmem_limit_bytes=mib << 20),
        **kw,
    )


def cost(us):
    return pl.CostEstimate(flops=int(us * 1e9), bytes_accessed=1 << 16, transcendentals=0)


def window_of(k, tile):
    low = BIN * k // tile * tile
    high = -(-BIN * (k + 1) // tile) * tile
    return low, high


def merge(parts, t, tile):
    bins = sorted({(8 * t) // BIN, (8 * t + 7) // BIN})
    out = None
    for k in bins:
        value = parts[k][..., 8 * t - window_of(k, tile)[0] :, :][..., :8, :]
        if out is None:
            out = value
        else:
            row = lax.broadcasted_iota(jnp.int32, value.shape, value.ndim - 2) + 8 * t
            out = jnp.where(row < BIN * k, out, value)
    return out


def spectra_kernel(f_ref, t_ref, o_ref):
    rows = []
    for j in range(NP):
        both = dot(t_ref[...], f_ref[j], 1, 1)
        rows.append(both[: 2 * NF] + both[2 * NF :])
    r = lax.broadcasted_iota(jnp.int32, (CH * ROWS, CH * ROWS), 0)
    q = (r * 43) >> 8
    rest = r - BIN * q
    source = ((q >> 3) * PC + (rest >> 1)) * 16 + (q & 7) * 2 + (rest & 1)
    move = (lax.broadcasted_iota(jnp.int32, r.shape, 1) == source).astype(F32).astype(BF)
    o_ref[...] = dot(move, jnp.concatenate(rows, axis=0).astype(BF)).astype(BF)


def swap_rows(x):
    even = lax.broadcasted_iota(jnp.int32, x.shape, 0) % 2 == 0
    n = x.shape[0]
    return jnp.where(even, -pltpu.roll(x, n - 1, 0), pltpu.roll(x, 1, 0))


def conv_kernel(f0, f1, f2, f3, r_ref, give, keep, l1, l2):
    x, zl, zh, y, c = place()
    for dx, ref in enumerate((f0, f1, f2, f3)):
        for dz in range(4):
            xb = lax.rem(x + 4 - dx, 4)
            zb = zl ^ dz
            yb = lax.rem(xb, 2) * 2 + zb // 2
            to = lax.rem(zb + c, 2) * 8 + lax.rem(yb + 4 - y, 4) * 2 + lax.rem(xb // 2 + zh, 2)
            rows = ref[dz].astype(F32)
            l1[to] = rows
            l2[to] = swap_rows(rows)

    sb = 256

    def step(i, carry):
        g, at = i // 4, pl.ds(pl.multiple_of(lax.rem(i, 4) * sb, sb), sb)
        parts = {}
        for k in range(4):
            low, high = window_of(k, 8)
            n = 16 * (high - low)
            rows = pl.ds(pl.multiple_of(g * 24, 8) + low, high - low)
            a1 = l1[:, rows].reshape(n, NR).astype(BF)
            a2 = l2[:, rows].reshape(n, NR).astype(BF)
            v = dot(a1, r_ref[0, 4 * g + k, at, :], 1, 1) + dot(a2, r_ref[1, 4 * g + k, at, :], 1, 1)
            parts[k] = v.reshape(16, high - low, sb)
        out = jnp.concatenate([merge(parts, t, 8) for t in range(3)], axis=1).astype(BF)
        keep[:, g, :, at] = out[:8]
        give[:, g, :, at] = out[8:]
        return carry

    lax.fori_loop(0, 2 * NS // sb, step, 0)


def convolve(pieces, reflection):
    give, keep = call(
        conv_kernel,
        [jax.ShapeDtypeStruct((8, 2, ROWS // 2, NS), BF)] * 2,
        "conv",
        in_specs=[pl.BlockSpec(memory_space=pltpu.VMEM)] * 5,
        scratch_shapes=[pltpu.VMEM((16, ROWS, NR), F32)] * 2,
        cost_estimate=cost(4),
    )(*pieces, reflection)
    return give.reshape(4, 2, ROWS, NS), keep.reshape(4, 2, ROWS, NS)


def window_kernel(p0, p1, p2, p3, r_ref, on_ref, a_ref, t_ref, w_ref, up_ref):
    steps = lax.broadcasted_iota(jnp.int32, (NT, NS), 0)

    def half(i, carry):
        e = 1 - i
        total = (p0[e].astype(F32) + p1[e].astype(F32)) + (p2[e].astype(F32) + p3[e].astype(F32))
        u = hi_lo_hi(total + r_ref[i].astype(F32), 0)
        acc = jnp.zeros((2 * ROWS, NS), F32)
        for j in range(PC):
            field = dot(a_ref[j], u)
            field = jnp.where(steps < on_ref[e, j : j + 1, :], field, 0.0).astype(BF)
            up_ref[j] = field
            acc += dot(t_ref[j], field)
        w_ref[e] = (acc[:ROWS] + acc[ROWS:]).astype(BF)
        return carry

    lax.fori_loop(0, 2, half, 0)


def flip_kernel(a_ref, b_ref, o_ref):
    for i, ref in enumerate((a_ref, b_ref)):
        for j in range(PC):
            o_ref[i * PC + j] = ref[j].T


def load_kernel(r_hbm, o_ref, sem):
    copies = [
        pltpu.make_async_copy(r_hbm.at[part, k], o_ref.at[part, k], sem.at[part, k])
        for k in range(NF)
        for part in range(2)
    ]
    for copy in copies:
        copy.start()
    for copy in copies:
        copy.wait()


def corr_kernel(w0, w1, w2, w3, v0, v1, v2, v3, r_ref, o0, o1, o2, o3, out, acc):
    x, zl, zh, y, c = place()
    refs = (w0, w1, w2, w3, v0, v1, v2, v3)
    row = lax.broadcasted_iota(jnp.int32, (256, NR), 0)
    even = row % 2 == 0

    def step(i, carry):
        for n in range(2):
            p = 2 * i + n
            t = (p >= 3).astype(jnp.int32) + (p >= 7).astype(jnp.int32)
            k = p - t
            at = pl.ds(pl.multiple_of(16 * t, 16), 16)
            m = jnp.concatenate([w[e, at] for w in refs for e in range(2)], axis=0)
            q = dot(m, r_ref[1, k])
            g = dot(m, r_ref[0, k]) + jnp.where(even, pltpu.roll(q, 255, 0), -pltpu.roll(q, 1, 0))
            mine = (row % 16 + 16 * t >= BIN * k) & (row % 16 + 16 * t < BIN * k + BIN)
            acc[t] = jnp.where(mine, g, acc[t])
        return carry

    lax.fori_loop(0, 5, step, 0)
    for i in range(16):
        other, d, e = i // 8, i // 2 % 4, i % 2
        yb = lax.rem(y + 4 - d, 4)
        xb = lax.rem(zh + e, 2) * 2 + yb // 2
        zb = lax.rem(yb, 2) * 2 + lax.rem(c + other, 2)
        out[lax.rem(xb + 4 - x, 4), zb ^ zl] = jnp.concatenate([acc[t, 16 * i : 16 * i + 16] for t in range(3)], axis=0).astype(BF)
    for d, ref in enumerate((o0, o1, o2, o3)):
        ref[...] = out[d]


def correlate(waves, reflection):
    return call(
        corr_kernel,
        [jax.ShapeDtypeStruct((4, ROWS, NR), BF)] * 4,
        "corr",
        in_specs=[pl.BlockSpec(memory_space=pltpu.VMEM)] * 9,
        scratch_shapes=[pltpu.VMEM((4, 4, ROWS, NR), BF), pltpu.VMEM((3, 256, NR), F32)],
        cost_estimate=cost(4),
        mib=16,
    )(*waves, reflection)


def sum_kernel(*refs):
    ins, (keep, *gives) = refs[: 4 * CH], refs[4 * CH :]
    for h in range(CH):
        g = ins[4 * h : 4 * h + 4]
        total = (g[0][...].astype(F32) + g[1][...].astype(F32)) + (g[2][...].astype(F32) + g[3][...].astype(F32))
        keep[h] = total[0]
        for d, give in enumerate(gives):
            give[h] = total[d + 1].astype(BF)


def refocus_kernel(g0, g1, g2, g3, d_ref, on_ref, a_ref, o_ref):
    steps = lax.broadcasted_iota(jnp.int32, (NR, NT), 1)
    for h in range(CH):
        g = (g0[h] + g1[h].astype(F32)) + (g2[h].astype(F32) + g3[h].astype(F32))
        gt = hi_lo_hi(g.T, 1)
        for i in range(PC):
            j = h * PC + i
            field = dot(gt, a_ref[i], 1, 1)
            field = jnp.where(steps < on_ref[:, j : j + 1], field, 0.0)
            o_ref[j] = d_ref[j].astype(F32) + field


def send(value, axis, to):
    return lax.ppermute(value, axis, [(i, to(i)) for i in range(16)])


def to_x(d):
    return lambda i: (i // 4 + d) % 4 * 4 + i % 4


def to_zl(d):
    return lambda i: i ^ d


def to_y(d):
    return lambda i: i // 8 * 8 + (i // 2 % 4 + d) % 4 * 2 + i % 2


def to_zh(i):
    return (i + 8) % 16


def to_core(i):
    return i ^ 1


def together(*lists):
    flat = lax.optimization_barrier(tuple(v for values in lists for v in values))
    out, at = [], 0
    for values in lists:
        out.append(list(flat[at : at + len(values)]))
        at += len(values)
    return out


def on_device(reflection, focusing, direct, onset_source, onset_receiver):
    t_spec = jnp.asarray(spectra_table())
    t_samp = jnp.asarray(samples_table())

    spectra = call(spectra_kernel, jax.ShapeDtypeStruct((CH * ROWS, NR), BF), "spectra")(
        focusing, jnp.asarray(trace_table())
    )
    rcv = lax.axis_index("rcv")
    near_far = [lax.dynamic_slice_in_dim(onset_source, r * NP, NP, 0) for r in (rcv, rcv ^ 8)]
    onsets = [jnp.stack([o[h * PC : (h + 1) * PC] for o in near_far]) for h in range(CH)]
    near = [spectra] + [send(spectra, "src", to_zl(d)) for d in (1, 2, 3)]
    stacks = [jnp.stack([n[h * ROWS : (h + 1) * ROWS] for n in near]) for h in range(CH)]
    [reflection], stacks[:1] = together([reflection], stacks[:1])
    pieces = [[stacks[0]] + [send(stacks[0], "src", to_x(d)) for d in (1, 2, 3)]]
    held = call(
        load_kernel,
        pltpu.VMEM((2, NF, NS, NR), BF),
        "load",
        in_specs=[pl.BlockSpec(memory_space=pltpu.HBM)],
        out_specs=pl.BlockSpec(memory_space=pltpu.VMEM),
        scratch_shapes=[pltpu.SemaphoreType.DMA((2, NF))],
        cost_estimate=cost(3),
        mib=50,
    )(reflection)

    def summed(give, keep):
        got = send(give, "rcv", to_core)
        return [(keep[d].astype(F32) + got[d].astype(F32)).astype(BF) for d in range(4)]

    def over_y(both):
        return [both[0]] + [send(both[d], "rcv", to_y(d)) for d in (1, 2, 3)]

    def half_sum(both):
        return ((both[0].astype(F32) + both[1].astype(F32)) + (both[2].astype(F32) + both[3].astype(F32))).astype(BF)

    def window(both, half, h):
        return call(
            window_kernel,
            (jax.ShapeDtypeStruct((2, ROWS, NS), BF), jax.ShapeDtypeStruct((PC, NT, NS), BF)),
            "window",
            cost_estimate=cost(2),
        )(*both, half, onsets[h], t_samp, t_spec)

    give_a, keep_a = convolve(pieces[0], held)
    [second], [keep_a] = together([stacks[1]], [keep_a])
    pieces.append([second] + [send(second, "src", to_x(d)) for d in (1, 2, 3)])
    sum_a = summed(give_a, keep_a)
    both_a = over_y(sum_a)
    pieces[1][1:], both_a[1:2] = together(pieces[1][1:], both_a[1:2])
    sum_b = summed(*convolve(pieces[1], held))
    both_a[1:], sum_b = together(both_a[1:], sum_b)
    both_b = over_y(sum_b)
    half_a = send(half_sum(both_a), "rcv", to_zh)
    half_b = send(half_sum(both_b), "rcv", to_zh)
    [half_a], both_b = together([half_a], both_b)
    wave_a, field_a = window(both_a, half_a, 0)
    wave_b, field_b = window(both_b, half_b, 1)
    own_a = over_y([wave_a] * 4)
    own_b = over_y([wave_b] * 4)
    upgoing = call(
        flip_kernel, jax.ShapeDtypeStruct((NP, NS, NT), BF), "flip", cost_estimate=cost(2)
    )(field_a, field_b)
    parts = []
    own_a[:1], [upgoing] = together(own_a[:1], [upgoing])

    def over_core(own):
        return [*own, *[send(w, "rcv", to_core) for w in own]]

    def over_x(back):
        return [back[0]] + [send(back[d], "src", to_x(d)) for d in (1, 2, 3)]

    parts_a = over_x(correlate(over_core(own_a), held))
    own_b[1:], parts_a = together(own_b[1:], parts_a)
    parts = parts_a + over_x(correlate(over_core(own_b), held))

    keep, *gives = call(
        sum_kernel,
        [jax.ShapeDtypeStruct((CH, ROWS, NR), F32)] + [jax.ShapeDtypeStruct((CH, ROWS, NR), BF)] * 3,
        "sum_x",
    )(*parts)
    last = [keep] + [send(gives[d - 1], "src", to_zl(d)) for d in (1, 2, 3)]
    refocused = call(refocus_kernel, jax.ShapeDtypeStruct((NP, NR, NT), F32), "refocus")(
        *last, direct, onset_receiver.T, t_samp
    )
    return (upgoing, refocused)


def solution(mesh):
    in_specs = (
        P(None, None, "src", "rcv"),
        P("src", "rcv", None),
        P("src", "rcv", None),
        P(None, "src"),
        P("src", "rcv"),
    )
    out_specs = (P("rcv", "src", None), P("src", "rcv", None))
    return jax.shard_map(
        on_device, mesh=mesh, in_specs=in_specs, out_specs=out_specs, check_vma=False
    )
```

```python
import functools
import math

import jax
import jax.numpy as jnp
import numpy as np
from jax import lax
from jax.experimental import pallas as pl
from jax.experimental.pallas import tpu as pltpu
from jax.sharding import PartitionSpec as P

NF = 8
NT = 128
NP = 6
PC = 3
CH = NP // PC
ROWS = 2 * NF * PC
BIN = 2 * PC
NS = 1024
NR = 256
BF = jnp.bfloat16
F32 = jnp.float32


def split(table):
    high = table.astype(BF)
    low = (table - high.astype(np.float32)).astype(BF)
    return high, low


def tables():
    k = np.arange(1, NF + 1)[:, None]
    t = np.arange(NT)[None, :]
    phase = 2.0 * math.pi / NT * ((k * t) % NT)
    return np.cos(phase).astype(np.float32), np.sin(phase).astype(np.float32)


def trace_table():
    cosines, sines = tables()
    return np.concatenate(split(np.stack([cosines, -sines], 1).reshape(2 * NF, NT)))


def spectra_table():
    cosines, sines = tables()
    full = np.zeros((PC, NF, PC, 2, NT), np.float32)
    for j in range(PC):
        full[j, :, j, 0] = cosines
        full[j, :, j, 1] = -sines
    return np.concatenate(split(full.reshape(PC, ROWS, NT)), axis=1)


def samples_table():
    cosines, sines = tables()
    full = np.zeros((PC, NT, NF, PC, 2), np.float32)
    for j in range(PC):
        full[j, :, :, j, 0] = 2.0 / NT * cosines.T
        full[j, :, :, j, 1] = -2.0 / NT * sines.T
    high, low = split(full.reshape(PC, NT, ROWS))
    return np.concatenate([high, high, low], axis=2)


def dot(a, b, ca=1, cb=0):
    return lax.dot_general(a, b, (((ca,), (cb,)), ((), ())), preferred_element_type=F32)


def hi_lo_hi(x, axis):
    high = x.astype(BF)
    low = (x - high.astype(F32)).astype(BF)
    return jnp.concatenate([high, low, high], axis=axis)


def place():
    src = lax.axis_index("src")
    rcv = lax.axis_index("rcv")
    return src // 4, src % 4, rcv // 8, (rcv // 2) % 4, rcv % 2


def call(kernel, out, name, mib=8, **kw):
    return pl.pallas_call(
        kernel,
        out_shape=out,
        name=name,
        compiler_params=pltpu.CompilerParams(vmem_limit_bytes=int(mib * 2**20)),
        **kw,
    )


def cost(us):
    return pl.CostEstimate(flops=int(us * 1e9), bytes_accessed=1 << 16, transcendentals=0)


def window_of(k, tile):
    low = BIN * k // tile * tile
    high = -(-BIN * (k + 1) // tile) * tile
    return low, high


def merge(parts, t, tile):
    bins = sorted({(8 * t) // BIN, (8 * t + 7) // BIN})
    out = None
    for k in bins:
        value = parts[k][..., 8 * t - window_of(k, tile)[0] :, :][..., :8, :]
        if out is None:
            out = value
        else:
            row = lax.broadcasted_iota(jnp.int32, value.shape, value.ndim - 2) + 8 * t
            out = jnp.where(row < BIN * k, out, value)
    return out


def spectra_kernel(f_hbm, t_hbm, o_ref, f_ref, t_ref, sem):
    copies = [pltpu.make_async_copy(f_hbm.at[j], f_ref.at[j], sem.at[j]) for j in range(NP)]
    copies.append(pltpu.make_async_copy(t_hbm, t_ref, sem.at[NP]))
    for copy in copies:
        copy.start()
    for copy in copies:
        copy.wait()
    rows = []
    for j in range(NP):
        both = dot(t_ref[...], f_ref[j], 1, 1)
        rows.append(both[: 2 * NF] + both[2 * NF :])
    r = lax.broadcasted_iota(jnp.int32, (CH * ROWS, CH * ROWS), 0)
    q = (r * 43) >> 8
    rest = r - BIN * q
    source = ((q >> 3) * PC + (rest >> 1)) * 16 + (q & 7) * 2 + (rest & 1)
    move = (lax.broadcasted_iota(jnp.int32, r.shape, 1) == source).astype(F32).astype(BF)
    o_ref[...] = dot(move, jnp.concatenate(rows, axis=0).astype(BF)).astype(BF)


def swap_rows(x):
    even = lax.broadcasted_iota(jnp.int32, x.shape, 0) % 2 == 0
    n = x.shape[0]
    return jnp.where(even, -pltpu.roll(x, n - 1, 0), pltpu.roll(x, 1, 0))


def conv_kernel(f0, f1, f2, f3, r_ref, give, keep, l1, l2):
    x, zl, zh, y, c = place()
    for dx, ref in enumerate((f0, f1, f2, f3)):
        for dz in range(4):
            xb = lax.rem(x + 4 - dx, 4)
            zb = zl ^ dz
            yb = lax.rem(xb, 2) * 2 + zb // 2
            to = lax.rem(zb + c, 2) * 8 + lax.rem(yb + 4 - y, 4) * 2 + lax.rem(xb // 2 + zh, 2)
            rows = ref[dz].astype(F32)
            l1[to] = rows
            l2[to] = swap_rows(rows)

    sb = 256

    def step(i, carry):
        g, at = i // 4, pl.ds(pl.multiple_of(lax.rem(i, 4) * sb, sb), sb)
        parts = {}
        for k in range(4):
            low, high = window_of(k, 8)
            n = 16 * (high - low)
            rows = pl.ds(pl.multiple_of(g * 24, 8) + low, high - low)
            a1 = l1[:, rows].reshape(n, NR).astype(BF)
            a2 = l2[:, rows].reshape(n, NR).astype(BF)
            v = dot(a1, r_ref[0, 4 * g + k, at, :], 1, 1) + dot(a2, r_ref[1, 4 * g + k, at, :], 1, 1)
            parts[k] = v.reshape(16, high - low, sb)
        out = jnp.concatenate([merge(parts, t, 8) for t in range(3)], axis=1).astype(BF)
        keep[:, g, :, at] = out[:8]
        give[:, g, :, at] = out[8:]
        return carry

    lax.fori_loop(0, 2 * NS // sb, step, 0)


def convolve(pieces, reflection):
    give, keep = call(
        conv_kernel,
        [jax.ShapeDtypeStruct((8, 2, ROWS // 2, NS), BF)] * 2,
        "conv",
        in_specs=[pl.BlockSpec(memory_space=pltpu.VMEM)] * 5,
        scratch_shapes=[pltpu.VMEM((16, ROWS, NR), F32)] * 2,
        cost_estimate=cost(4),
    )(*pieces, reflection)
    return give.reshape(4, 2, ROWS, NS), keep.reshape(4, 2, ROWS, NS)


def window_kernel(p0, p1, p2, p3, r_ref, on_ref, a_ref, t_ref, w_ref, up_ref):
    steps = lax.broadcasted_iota(jnp.int32, (NT, NS), 0)

    def half(i, carry):
        e = 1 - i
        total = (p0[e].astype(F32) + p1[e].astype(F32)) + (p2[e].astype(F32) + p3[e].astype(F32))
        u = hi_lo_hi(total + r_ref[i].astype(F32), 0)
        acc = jnp.zeros((2 * ROWS, NS), F32)
        for j in range(PC):
            field = dot(a_ref[j], u)
            field = jnp.where(steps < on_ref[e, j : j + 1, :], field, 0.0).astype(BF)
            up_ref[j] = field
            acc += dot(t_ref[j], field)
        w_ref[e] = (acc[:ROWS] + acc[ROWS:]).astype(BF)
        return carry

    lax.fori_loop(0, 2, half, 0)


def flip_kernel(a_ref, b_ref, o_ref):
    for i, ref in enumerate((a_ref, b_ref)):
        for j in range(PC):
            o_ref[i * PC + j] = ref[j].T


def load_kernel(r_hbm, o_ref, sem):
    copies = [
        pltpu.make_async_copy(r_hbm.at[part, k], o_ref.at[part, k], sem.at[part, k])
        for k in range(NF)
        for part in range(2)
    ]
    for copy in copies:
        copy.start()
    for copy in copies:
        copy.wait()


def corr_kernel(w0, w1, w2, w3, v0, v1, v2, v3, r_ref, *rest):
    *firsts, o0, o1, o2, o3, out, acc = rest
    x, zl, zh, y, c = place()
    refs = (w0, w1, w2, w3, v0, v1, v2, v3)
    row = lax.broadcasted_iota(jnp.int32, (256, NR), 0)
    even = row % 2 == 0

    def step(i, carry):
        for n in range(5):
            p = 5 * i + n
            t = (p >= 3).astype(jnp.int32) + (p >= 7).astype(jnp.int32)
            k = p - t
            at = pl.ds(pl.multiple_of(16 * t, 16), 16)
            m = jnp.concatenate([w[e, at] for w in refs for e in range(2)], axis=0)
            q = dot(m, r_ref[1, k])
            g = dot(m, r_ref[0, k]) + jnp.where(even, pltpu.roll(q, 255, 0), -pltpu.roll(q, 1, 0))
            mine = (row % 16 + 16 * t >= BIN * k) & (row % 16 + 16 * t < BIN * k + BIN)
            acc[t] = jnp.where(mine, g, acc[t])
        return carry

    lax.fori_loop(0, 2, step, 0)
    for i in range(16):
        other, d, e = i // 8, i // 2 % 4, i % 2
        yb = lax.rem(y + 4 - d, 4)
        xb = lax.rem(zh + e, 2) * 2 + yb // 2
        zb = lax.rem(yb, 2) * 2 + lax.rem(c + other, 2)
        out[lax.rem(xb + 4 - x, 4), zb ^ zl] = jnp.concatenate([acc[t, 16 * i : 16 * i + 16] for t in range(3)], axis=0).astype(BF)
    for d, ref in enumerate((o0, o1, o2, o3)):
        if firsts:
            ref[0] = firsts[d][...]
            ref[1] = out[d]
        else:
            ref[...] = out[d]


def correlate(waves, reflection, firsts=()):
    shape = (4, ROWS, NR) if not firsts else (2, 4, ROWS, NR)
    return call(
        corr_kernel,
        [jax.ShapeDtypeStruct(shape, BF)] * 4,
        "corr",
        in_specs=[pl.BlockSpec(memory_space=pltpu.VMEM)] * (9 + len(firsts)),
        scratch_shapes=[pltpu.VMEM((4, 4, ROWS, NR), BF), pltpu.VMEM((3, 256, NR), F32)],
        cost_estimate=cost(4),
        mib=16,
    )(*waves, reflection, *firsts)


def sum_kernel(g0, g1, g2, g3, keep, *gives):
    for h in range(CH):
        total = (g0[h].astype(F32) + g1[h].astype(F32)) + (g2[h].astype(F32) + g3[h].astype(F32))
        keep[h] = total[0]
        for d, give in enumerate(gives):
            give[h] = total[d + 1].astype(BF)


def refocus_kernel(g0, g1, g2, g3, d_ref, on_ref, a_ref, o_ref):
    steps = lax.broadcasted_iota(jnp.int32, (NR, NT), 1)
    for h in range(CH):
        g = (g0[h] + g1[h].astype(F32)) + (g2[h].astype(F32) + g3[h].astype(F32))
        gt = hi_lo_hi(g.T, 1)
        for i in range(PC):
            j = h * PC + i
            field = dot(gt, a_ref[i], 1, 1)
            field = jnp.where(steps < on_ref[:, j : j + 1], field, 0.0)
            o_ref[j] = d_ref[j].astype(F32) + field


def send(value, axis, to):
    return lax.ppermute(value, axis, [(i, to(i)) for i in range(16)])


def to_x(d):
    return lambda i: (i // 4 + d) % 4 * 4 + i % 4


def to_zl(d):
    return lambda i: i ^ d


def to_y(d):
    return lambda i: i // 8 * 8 + (i // 2 % 4 + d) % 4 * 2 + i % 2


def to_zh(i):
    return (i + 8) % 16


def to_core(i):
    return i ^ 1


def together(*lists):
    flat = lax.optimization_barrier(tuple(v for values in lists for v in values))
    out, at = [], 0
    for values in lists:
        out.append(list(flat[at : at + len(values)]))
        at += len(values)
    return out


def on_device(reflection, focusing, direct, onset_source, onset_receiver):
    t_spec = jnp.asarray(spectra_table())
    t_samp = jnp.asarray(samples_table())

    spectra = call(spectra_kernel, pltpu.VMEM((CH * ROWS, NR), BF), "spectra", mib=62,
        out_specs=pl.BlockSpec(memory_space=pltpu.VMEM),
        in_specs=[pl.BlockSpec(memory_space=pltpu.HBM)] * 2,
        scratch_shapes=[
            pltpu.VMEM((NP, NR, NT), BF),
            pltpu.VMEM((4 * NF, NT), BF),
            pltpu.SemaphoreType.DMA((NP + 1,)),
        ],
    )(
        focusing, jnp.asarray(trace_table())
    )
    rcv = lax.axis_index("rcv")
    near_far = [lax.dynamic_slice_in_dim(onset_source, r * NP, NP, 0) for r in (rcv, rcv ^ 8)]
    onsets = [jnp.stack([o[h * PC : (h + 1) * PC] for o in near_far]) for h in range(CH)]
    near = [send(spectra, "src", to_zl(d)) for d in (1, 2, 3)]
    held = call(
        load_kernel,
        pltpu.VMEM((2, NF, NS, NR), BF),
        "load",
        in_specs=[pl.BlockSpec(memory_space=pltpu.HBM)],
        out_specs=pl.BlockSpec(memory_space=pltpu.VMEM),
        scratch_shapes=[pltpu.SemaphoreType.DMA((2, NF))],
        cost_estimate=cost(3),
        mib=50,
    )(reflection)
    near, [spectra, held] = together(near, [spectra, held])
    near = [spectra, *near]
    stacks = [jnp.stack([n[h * ROWS : (h + 1) * ROWS] for n in near]) for h in range(CH)]
    pieces = [[stacks[0]] + [send(stacks[0], "src", to_x(d)) for d in (1, 2, 3)]]

    def summed(give, keep):
        got = send(give, "rcv", to_core)
        return [(keep[d].astype(F32) + got[d].astype(F32)).astype(BF) for d in range(4)]

    def over_y(both):
        return [both[0]] + [send(both[d], "rcv", to_y(d)) for d in (1, 2, 3)]

    def half_sum(both):
        return ((both[0].astype(F32) + both[1].astype(F32)) + (both[2].astype(F32) + both[3].astype(F32))).astype(BF)

    def window(both, half, h):
        return call(
            window_kernel,
            (jax.ShapeDtypeStruct((2, ROWS, NS), BF), jax.ShapeDtypeStruct((PC, NT, NS), BF)),
            "window",
            cost_estimate=cost(2),
        )(*both, half, onsets[h], t_samp, t_spec)

    give_a, keep_a = convolve(pieces[0], held)
    [second], [keep_a] = together([stacks[1]], [keep_a])
    pieces.append([second] + [send(second, "src", to_x(d)) for d in (1, 2, 3)])
    sum_a = summed(give_a, keep_a)
    pieces[1][1:], sum_a = together(pieces[1][1:], sum_a)
    both_a = over_y(sum_a)
    sum_b = summed(*convolve(pieces[1], held))
    both_a[1:], sum_b = together(both_a[1:], sum_b)
    both_b = over_y(sum_b)
    half_a = send(half_sum(both_a), "rcv", to_zh)
    half_b = send(half_sum(both_b), "rcv", to_zh)
    [half_a], both_b = together([half_a], both_b)
    wave_a, field_a = window(both_a, half_a, 0)
    wave_b, field_b = window(both_b, half_b, 1)
    own_a = over_y([wave_a] * 4)
    own_b = over_y([wave_b] * 4)
    upgoing = call(
        flip_kernel, jax.ShapeDtypeStruct((NP, NS, NT), BF), "flip", cost_estimate=cost(2)
    )(field_a, field_b)
    parts = []
    own_a[:1], [upgoing] = together(own_a[:1], [upgoing])

    def over_core(own):
        return [*own, *[send(w, "rcv", to_core) for w in own]]

    def over_x(back):
        return [back[0]] + [send(back[d], "src", to_x(d)) for d in (1, 2, 3)]

    back_a = list(correlate(over_core(own_a), held))
    own_b[1:], back_a = together(own_b[1:], back_a)
    parts = over_x(correlate(over_core(own_b), held, back_a))

    keep, *gives = call(
        sum_kernel,
        [jax.ShapeDtypeStruct((CH, ROWS, NR), F32)] + [jax.ShapeDtypeStruct((CH, ROWS, NR), BF)] * 3,
        "sum_x",
    )(*parts)
    last = [keep] + [send(gives[d - 1], "src", to_zl(d)) for d in (1, 2, 3)]
    refocused = call(refocus_kernel, jax.ShapeDtypeStruct((NP, NR, NT), F32), "refocus")(
        *last, direct, onset_receiver.T, t_samp
    )
    return (upgoing, refocused)


def solution(mesh):
    in_specs = (
        P(None, None, "src", "rcv"),
        P("src", "rcv", None),
        P("src", "rcv", None),
        P(None, "src"),
        P("src", "rcv"),
    )
    out_specs = (P("rcv", "src", None), P("src", "rcv", None))
    return jax.shard_map(
        on_device, mesh=mesh, in_specs=in_specs, out_specs=out_specs, check_vma=False
    )
```

```python
import functools
import math

import jax
import jax.numpy as jnp
import numpy as np
from jax import lax
from jax.experimental import pallas as pl
from jax.experimental.pallas import tpu as pltpu
from jax.sharding import PartitionSpec as P

NF = 8
NT = 128
NP = 6
PC = 3
CH = NP // PC
ROWS = 2 * NF * PC
BIN = 2 * PC
NS = 1024
NR = 256
BF = jnp.bfloat16
F32 = jnp.float32


def split(table):
    high = table.astype(BF)
    low = (table - high.astype(np.float32)).astype(BF)
    return high, low


def tables():
    k = np.arange(1, NF + 1)[:, None]
    t = np.arange(NT)[None, :]
    phase = 2.0 * math.pi / NT * ((k * t) % NT)
    return np.cos(phase).astype(np.float32), np.sin(phase).astype(np.float32)


def trace_table():
    cosines, sines = tables()
    return np.concatenate(split(np.stack([cosines, -sines], 1).reshape(2 * NF, NT)))


def spectra_table():
    cosines, sines = tables()
    full = np.zeros((PC, NF, PC, 2, NT), np.float32)
    for j in range(PC):
        full[j, :, j, 0] = cosines
        full[j, :, j, 1] = -sines
    return np.concatenate(split(full.reshape(PC, ROWS, NT)), axis=1)


def samples_table():
    cosines, sines = tables()
    full = np.zeros((PC, NT, NF, PC, 2), np.float32)
    for j in range(PC):
        full[j, :, :, j, 0] = 2.0 / NT * cosines.T
        full[j, :, :, j, 1] = -2.0 / NT * sines.T
    high, low = split(full.reshape(PC, NT, ROWS))
    return np.concatenate([high, high, low], axis=2)


def dot(a, b, ca=1, cb=0):
    return lax.dot_general(a, b, (((ca,), (cb,)), ((), ())), preferred_element_type=F32)


def hi_lo_hi(x, axis):
    high = x.astype(BF)
    low = (x - high.astype(F32)).astype(BF)
    return jnp.concatenate([high, low, high], axis=axis)


def place():
    src = lax.axis_index("src")
    rcv = lax.axis_index("rcv")
    return src // 4, src % 4, rcv // 8, (rcv // 2) % 4, rcv % 2


def call(kernel, out, name, mib=8, **kw):
    return pl.pallas_call(
        kernel,
        out_shape=out,
        name=name,
        compiler_params=pltpu.CompilerParams(vmem_limit_bytes=int(mib * 2**20)),
        **kw,
    )


def cost(us):
    return pl.CostEstimate(flops=int(us * 1e9), bytes_accessed=1 << 16, transcendentals=0)


def window_of(k, tile):
    low = BIN * k // tile * tile
    high = -(-BIN * (k + 1) // tile) * tile
    return low, high


def merge(parts, t, tile):
    bins = sorted({(8 * t) // BIN, (8 * t + 7) // BIN})
    out = None
    for k in bins:
        value = parts[k][..., 8 * t - window_of(k, tile)[0] :, :][..., :8, :]
        if out is None:
            out = value
        else:
            row = lax.broadcasted_iota(jnp.int32, value.shape, value.ndim - 2) + 8 * t
            out = jnp.where(row < BIN * k, out, value)
    return out


def spectra_kernel(f_hbm, t_hbm, o_ref, f_ref, t_ref, sem):
    copies = [pltpu.make_async_copy(f_hbm.at[j], f_ref.at[j], sem.at[j]) for j in range(NP)]
    copies.append(pltpu.make_async_copy(t_hbm, t_ref, sem.at[NP]))
    for copy in copies:
        copy.start()
    for copy in copies:
        copy.wait()
    rows = []
    for j in range(NP):
        both = dot(t_ref[...], f_ref[j], 1, 1)
        rows.append(both[: 2 * NF] + both[2 * NF :])
    r = lax.broadcasted_iota(jnp.int32, (CH * ROWS, CH * ROWS), 0)
    q = (r * 43) >> 8
    rest = r - BIN * q
    source = ((q >> 3) * PC + (rest >> 1)) * 16 + (q & 7) * 2 + (rest & 1)
    move = (lax.broadcasted_iota(jnp.int32, r.shape, 1) == source).astype(F32).astype(BF)
    o_ref[...] = dot(move, jnp.concatenate(rows, axis=0).astype(BF)).astype(BF)


def swap_rows(x):
    even = lax.broadcasted_iota(jnp.int32, x.shape, 0) % 2 == 0
    n = x.shape[0]
    return jnp.where(even, -pltpu.roll(x, n - 1, 0), pltpu.roll(x, 1, 0))


def conv_kernel(chunk, f0, f1, f2, f3, r_ref, give, keep, l1, l2):
    x, zl, zh, y, c = place()
    for dx, ref in enumerate((f0, f1, f2, f3)):
        for dz in range(4):
            xb = lax.rem(x + 4 - dx, 4)
            zb = zl ^ dz
            yb = lax.rem(xb, 2) * 2 + zb // 2
            to = lax.rem(zb + c, 2) * 8 + lax.rem(yb + 4 - y, 4) * 2 + lax.rem(xb // 2 + zh, 2)
            rows = ref[dz, chunk * ROWS : (chunk + 1) * ROWS].astype(F32)
            l1[to] = rows
            l2[to] = swap_rows(rows)

    sb = 256

    def step(i, carry):
        g, at = i // 4, pl.ds(pl.multiple_of(lax.rem(i, 4) * sb, sb), sb)
        parts = {}
        for k in range(4):
            low, high = window_of(k, 8)
            n = 16 * (high - low)
            rows = pl.ds(pl.multiple_of(g * 24, 8) + low, high - low)
            a1 = l1[:, rows].reshape(n, NR).astype(BF)
            a2 = l2[:, rows].reshape(n, NR).astype(BF)
            v = dot(a1, r_ref[0, 4 * g + k, at, :], 1, 1) + dot(a2, r_ref[1, 4 * g + k, at, :], 1, 1)
            parts[k] = v.reshape(16, high - low, sb)
        out = jnp.concatenate([merge(parts, t, 8) for t in range(3)], axis=1).astype(BF)
        keep[:, g, :, at] = out[:8]
        give[:, g, :, at] = out[8:]
        return carry

    lax.fori_loop(0, 2 * NS // sb, step, 0)


def convolve(pieces, reflection, chunk):
    give, keep = call(
        functools.partial(conv_kernel, chunk),
        [jax.ShapeDtypeStruct((8, 2, ROWS // 2, NS), BF)] * 2,
        f"conv{chunk}",
        in_specs=[pl.BlockSpec(memory_space=pltpu.VMEM)] * 5,
        scratch_shapes=[pltpu.VMEM((16, ROWS, NR), F32)] * 2,
        cost_estimate=cost(4),
    )(*pieces, reflection)
    return give.reshape(4, 2, ROWS, NS), keep.reshape(4, 2, ROWS, NS)


def window_kernel(chunk, p0, p1, p2, p3, r_ref, on_ref, a_ref, t_ref, w_ref, up_ref):
    steps = lax.broadcasted_iota(jnp.int32, (NT, NS), 0)

    def half(i, carry):
        e = 1 - i
        first = lax.rem(lax.axis_index("rcv") + 8 * e, 16) * NP + chunk * PC
        total = (p0[e].astype(F32) + p1[e].astype(F32)) + (p2[e].astype(F32) + p3[e].astype(F32))
        u = hi_lo_hi(total + r_ref[i].astype(F32), 0)
        acc = jnp.zeros((2 * ROWS, NS), F32)
        for j in range(PC):
            field = dot(a_ref[j], u)
            field = jnp.where(steps < on_ref[pl.ds(first + j, 1), :], field, 0.0).astype(BF)
            up_ref[j] = field
            acc += dot(t_ref[j], field)
        w_ref[e] = (acc[:ROWS] + acc[ROWS:]).astype(BF)
        return carry

    lax.fori_loop(0, 2, half, 0)


def flip_kernel(a_ref, b_ref, o_ref):
    for i, ref in enumerate((a_ref, b_ref)):
        for j in range(PC):
            o_ref[i * PC + j] = ref[j].T


def load_kernel(r_hbm, o_ref, sem):
    copies = [
        pltpu.make_async_copy(r_hbm.at[part, k], o_ref.at[part, k], sem.at[part, k])
        for k in range(NF)
        for part in range(2)
    ]
    for copy in copies:
        copy.start()
    for copy in copies:
        copy.wait()


def corr_kernel(w0, w1, w2, w3, v0, v1, v2, v3, r_ref, o0, o1, o2, o3, out, acc):
    x, zl, zh, y, c = place()
    refs = (w0, w1, w2, w3, v0, v1, v2, v3)
    row = lax.broadcasted_iota(jnp.int32, (256, NR), 0)
    even = row % 2 == 0

    def step(i, carry):
        for n in range(5):
            p = 5 * i + n
            t = (p >= 3).astype(jnp.int32) + (p >= 7).astype(jnp.int32)
            k = p - t
            at = pl.ds(pl.multiple_of(16 * t, 16), 16)
            m = jnp.concatenate([w[e, at] for w in refs for e in range(2)], axis=0)
            q = dot(m, r_ref[1, k])
            g = dot(m, r_ref[0, k]) + jnp.where(even, pltpu.roll(q, 255, 0), -pltpu.roll(q, 1, 0))
            mine = (row % 16 + 16 * t >= BIN * k) & (row % 16 + 16 * t < BIN * k + BIN)
            acc[t] = jnp.where(mine, g, acc[t])
        return carry

    lax.fori_loop(0, 2, step, 0)
    for i in range(16):
        other, d, e = i // 8, i // 2 % 4, i % 2
        yb = lax.rem(y + 4 - d, 4)
        xb = lax.rem(zh + e, 2) * 2 + yb // 2
        zb = lax.rem(yb, 2) * 2 + lax.rem(c + other, 2)
        out[lax.rem(xb + 4 - x, 4), zb ^ zl] = jnp.concatenate([acc[t, 16 * i : 16 * i + 16] for t in range(3)], axis=0).astype(BF)
    for d, ref in enumerate((o0, o1, o2, o3)):
        ref[...] = out[d]


def correlate(waves, reflection):
    return call(
        corr_kernel,
        [jax.ShapeDtypeStruct((4, ROWS, NR), BF)] * 4,
        "corr",
        in_specs=[pl.BlockSpec(memory_space=pltpu.VMEM)] * 9,
        scratch_shapes=[pltpu.VMEM((4, 4, ROWS, NR), BF), pltpu.VMEM((3, 256, NR), F32)],
        cost_estimate=cost(4),
        mib=16,
    )(*waves, reflection)


def sum_kernel(*refs):
    ins, (keep, *gives) = refs[: 4 * CH], refs[4 * CH :]
    for h in range(CH):
        g = ins[4 * h : 4 * h + 4]
        total = (g[0][...].astype(F32) + g[1][...].astype(F32)) + (g[2][...].astype(F32) + g[3][...].astype(F32))
        keep[h] = total[0]
        for d, give in enumerate(gives):
            give[h] = total[d + 1].astype(BF)


def refocus_kernel(g0, g1, g2, g3, d_ref, on_ref, a_ref, o_ref):
    steps = lax.broadcasted_iota(jnp.int32, (NR, NT), 1)
    for h in range(CH):
        g = (g0[h] + g1[h].astype(F32)) + (g2[h].astype(F32) + g3[h].astype(F32))
        gt = hi_lo_hi(g.T, 1)
        for i in range(PC):
            j = h * PC + i
            field = dot(gt, a_ref[i], 1, 1)
            field = jnp.where(steps < on_ref[:, j : j + 1], field, 0.0)
            o_ref[j] = d_ref[j].astype(F32) + field


def send(value, axis, to):
    return lax.ppermute(value, axis, [(i, to(i)) for i in range(16)])


def to_x(d):
    return lambda i: (i // 4 + d) % 4 * 4 + i % 4


def to_zl(d):
    return lambda i: i ^ d


def to_y(d):
    return lambda i: i // 8 * 8 + (i // 2 % 4 + d) % 4 * 2 + i % 2


def to_zh(i):
    return (i + 8) % 16


def to_core(i):
    return i ^ 1


def together(*lists):
    flat = lax.optimization_barrier(tuple(v for values in lists for v in values))
    out, at = [], 0
    for values in lists:
        out.append(list(flat[at : at + len(values)]))
        at += len(values)
    return out


def on_device(reflection, focusing, direct, onset_source, onset_receiver):
    t_spec = jnp.asarray(spectra_table())
    t_samp = jnp.asarray(samples_table())

    spectra = call(spectra_kernel, pltpu.VMEM((CH * ROWS, NR), BF), "spectra", mib=62,
        out_specs=pl.BlockSpec(memory_space=pltpu.VMEM),
        in_specs=[pl.BlockSpec(memory_space=pltpu.HBM)] * 2,
        scratch_shapes=[
            pltpu.VMEM((NP, NR, NT), BF),
            pltpu.VMEM((4 * NF, NT), BF),
            pltpu.SemaphoreType.DMA((NP + 1,)),
        ],
    )(
        focusing, jnp.asarray(trace_table())
    )
    near = [send(spectra, "src", to_zl(d)) for d in (1, 2, 3)]
    held = call(
        load_kernel,
        pltpu.VMEM((2, NF, NS, NR), BF),
        "load",
        in_specs=[pl.BlockSpec(memory_space=pltpu.HBM)],
        out_specs=pl.BlockSpec(memory_space=pltpu.VMEM),
        scratch_shapes=[pltpu.SemaphoreType.DMA((2, NF))],
        cost_estimate=cost(3),
        mib=50,
    )(reflection)
    near, [spectra, held] = together(near, [spectra, held])
    stack = jnp.stack([spectra, *near])
    pieces = [stack] + [send(stack, "src", to_x(d)) for d in (1, 2, 3)]

    def summed(give, keep):
        got = send(give, "rcv", to_core)
        return [(keep[d].astype(F32) + got[d].astype(F32)).astype(BF) for d in range(4)]

    def over_y(both):
        return [both[0]] + [send(both[d], "rcv", to_y(d)) for d in (1, 2, 3)]

    def half_sum(both):
        return ((both[0].astype(F32) + both[1].astype(F32)) + (both[2].astype(F32) + both[3].astype(F32))).astype(BF)

    def window(both, half, h):
        return call(
            functools.partial(window_kernel, h),
            (jax.ShapeDtypeStruct((2, ROWS, NS), BF), jax.ShapeDtypeStruct((PC, NT, NS), BF)),
            f"window{h}",
            cost_estimate=cost(2),
        )(*both, half, onset_source, t_samp, t_spec)

    sum_a = summed(*convolve(pieces, held, 0))
    both_a = over_y(sum_a)
    sum_b = summed(*convolve(pieces, held, 1))
    both_a[1:], sum_b = together(both_a[1:], sum_b)
    both_b = over_y(sum_b)
    half_a = send(half_sum(both_a), "rcv", to_zh)
    half_b = send(half_sum(both_b), "rcv", to_zh)
    [half_a], both_b = together([half_a], both_b)
    wave_a, field_a = window(both_a, half_a, 0)
    wave_b, field_b = window(both_b, half_b, 1)
    own_a = over_y([wave_a] * 4)
    own_b = over_y([wave_b] * 4)
    upgoing = call(
        flip_kernel, jax.ShapeDtypeStruct((NP, NS, NT), BF), "flip", cost_estimate=cost(2)
    )(field_a, field_b)
    parts = []
    own_a[:1], [upgoing] = together(own_a[:1], [upgoing])

    def over_core(own):
        return [*own, *[send(w, "rcv", to_core) for w in own]]

    def over_x(back):
        return [back[0]] + [send(back[d], "src", to_x(d)) for d in (1, 2, 3)]

    parts_a = over_x(correlate(over_core(own_a), held))
    own_b[1:3], parts_a[:1] = together(own_b[1:3], parts_a[:1])
    own_b[3:], parts_a[2:3] = together(own_b[3:], parts_a[2:3])
    parts = parts_a + over_x(correlate(over_core(own_b), held))

    keep, *gives = call(
        sum_kernel,
        [jax.ShapeDtypeStruct((CH, ROWS, NR), F32)] + [jax.ShapeDtypeStruct((CH, ROWS, NR), BF)] * 3,
        "sum_x",
    )(*parts)
    last = [keep] + [send(gives[d - 1], "src", to_zl(d)) for d in (1, 2, 3)]
    refocused = call(refocus_kernel, jax.ShapeDtypeStruct((NP, NR, NT), F32), "refocus")(
        *last, direct, onset_receiver.T, t_samp
    )
    return (upgoing, refocused)


def solution(mesh):
    in_specs = (
        P(None, None, "src", "rcv"),
        P("src", "rcv", None),
        P("src", "rcv", None),
        P(None, "src"),
        P("src", "rcv"),
    )
    out_specs = (P("rcv", "src", None), P("src", "rcv", None))
    return jax.shard_map(
        on_device, mesh=mesh, in_specs=in_specs, out_specs=out_specs, check_vma=False
    )
```

```python
import functools
import math

import jax
import jax.numpy as jnp
import numpy as np
from jax import lax
from jax.experimental import pallas as pl
from jax.experimental.pallas import tpu as pltpu
from jax.sharding import PartitionSpec as P

NF = 8
NT = 128
NP = 6
PC = 3
CH = NP // PC
ROWS = 2 * NF * PC
BIN = 2 * PC
NS = 1024
NR = 256
BF = jnp.bfloat16
F32 = jnp.float32


def split(table):
    high = table.astype(BF)
    low = (table - high.astype(np.float32)).astype(BF)
    return high, low


def tables():
    k = np.arange(1, NF + 1)[:, None]
    t = np.arange(NT)[None, :]
    phase = 2.0 * math.pi / NT * ((k * t) % NT)
    return np.cos(phase).astype(np.float32), np.sin(phase).astype(np.float32)


def trace_table():
    cosines, sines = tables()
    return np.concatenate(split(np.stack([cosines, -sines], 1).reshape(2 * NF, NT)))


def spectra_table():
    cosines, sines = tables()
    full = np.zeros((PC, NF, PC, 2, NT), np.float32)
    for j in range(PC):
        full[j, :, j, 0] = cosines
        full[j, :, j, 1] = -sines
    return np.concatenate(split(full.reshape(PC, ROWS, NT)), axis=1)


def samples_table():
    cosines, sines = tables()
    full = np.zeros((PC, NT, NF, PC, 2), np.float32)
    for j in range(PC):
        full[j, :, :, j, 0] = 2.0 / NT * cosines.T
        full[j, :, :, j, 1] = -2.0 / NT * sines.T
    high, low = split(full.reshape(PC, NT, ROWS))
    return np.concatenate([high, high, low], axis=2)


def dot(a, b, ca=1, cb=0):
    return lax.dot_general(a, b, (((ca,), (cb,)), ((), ())), preferred_element_type=F32)


def hi_lo_hi(x, axis):
    high = x.astype(BF)
    low = (x - high.astype(F32)).astype(BF)
    return jnp.concatenate([high, low, high], axis=axis)


def place():
    src = lax.axis_index("src")
    rcv = lax.axis_index("rcv")
    return src // 4, src % 4, rcv // 8, (rcv // 2) % 4, rcv % 2


def call(kernel, out, name, mib=8, **kw):
    return pl.pallas_call(
        kernel,
        out_shape=out,
        name=name,
        compiler_params=pltpu.CompilerParams(vmem_limit_bytes=int(mib * 2**20)),
        **kw,
    )


def cost(us):
    return pl.CostEstimate(flops=int(us * 1e9), bytes_accessed=1 << 16, transcendentals=0)


def window_of(k, tile):
    low = BIN * k // tile * tile
    high = -(-BIN * (k + 1) // tile) * tile
    return low, high


def merge(parts, t, tile):
    bins = sorted({(8 * t) // BIN, (8 * t + 7) // BIN})
    out = None
    for k in bins:
        value = parts[k][..., 8 * t - window_of(k, tile)[0] :, :][..., :8, :]
        if out is None:
            out = value
        else:
            row = lax.broadcasted_iota(jnp.int32, value.shape, value.ndim - 2) + 8 * t
            out = jnp.where(row < BIN * k, out, value)
    return out


def spectra_kernel(f_hbm, t_hbm, o_ref, f_ref, t_ref, sem):
    copies = [pltpu.make_async_copy(f_hbm.at[j], f_ref.at[j], sem.at[j]) for j in range(NP)]
    copies.append(pltpu.make_async_copy(t_hbm, t_ref, sem.at[NP]))
    for copy in copies:
        copy.start()
    for copy in copies:
        copy.wait()
    rows = []
    for j in range(NP):
        both = dot(t_ref[...], f_ref[j], 1, 1)
        rows.append(both[: 2 * NF] + both[2 * NF :])
    r = lax.broadcasted_iota(jnp.int32, (CH * ROWS, CH * ROWS), 0)
    q = (r * 43) >> 8
    rest = r - BIN * q
    source = ((q >> 3) * PC + (rest >> 1)) * 16 + (q & 7) * 2 + (rest & 1)
    move = (lax.broadcasted_iota(jnp.int32, r.shape, 1) == source).astype(F32).astype(BF)
    o_ref[...] = dot(move, jnp.concatenate(rows, axis=0).astype(BF)).astype(BF)


def swap_rows(x):
    even = lax.broadcasted_iota(jnp.int32, x.shape, 0) % 2 == 0
    n = x.shape[0]
    return jnp.where(even, -pltpu.roll(x, n - 1, 0), pltpu.roll(x, 1, 0))


def conv_kernel(chunk, f0, f1, f2, f3, r_ref, give, keep, l1, l2):
    x, zl, zh, y, c = place()
    for dx, ref in enumerate((f0, f1, f2, f3)):
        for dz in range(4):
            xb = lax.rem(x + 4 - dx, 4)
            zb = zl ^ dz
            yb = lax.rem(xb, 2) * 2 + zb // 2
            to = lax.rem(zb + c, 2) * 8 + lax.rem(yb + 4 - y, 4) * 2 + lax.rem(xb // 2 + zh, 2)
            rows = ref[dz, chunk * ROWS : (chunk + 1) * ROWS].astype(F32)
            l1[to] = rows
            l2[to] = swap_rows(rows)

    sb = 1024

    def step(i, carry):
        g, at = i, slice(None)
        parts = {}
        for k in range(4):
            low, high = window_of(k, 8)
            n = 16 * (high - low)
            rows = pl.ds(pl.multiple_of(g * 24, 8) + low, high - low)
            a1 = l1[:, rows].reshape(n, NR).astype(BF)
            a2 = l2[:, rows].reshape(n, NR).astype(BF)
            v = dot(a1, r_ref[0, 4 * g + k, at, :], 1, 1) + dot(a2, r_ref[1, 4 * g + k, at, :], 1, 1)
            parts[k] = v.reshape(16, high - low, sb)
        out = jnp.concatenate([merge(parts, t, 8) for t in range(3)], axis=1).astype(BF)
        keep[:, g, :, at] = out[:8]
        give[:, g, :, at] = out[8:]
        return carry

    lax.fori_loop(0, 2 * NS // sb, step, 0)


def convolve(pieces, reflection, chunk):
    give, keep = call(
        functools.partial(conv_kernel, chunk),
        [jax.ShapeDtypeStruct((8, 2, ROWS // 2, NS), BF)] * 2,
        f"conv{chunk}",
        in_specs=[pl.BlockSpec(memory_space=pltpu.VMEM)] * 5,
        scratch_shapes=[pltpu.VMEM((16, ROWS, NR), F32)] * 2,
        cost_estimate=cost(4),
    )(*pieces, reflection)
    return give.reshape(4, 2, ROWS, NS), keep.reshape(4, 2, ROWS, NS)


def window_kernel(chunk, p0, p1, p2, p3, r_ref, on_ref, a_ref, t_ref, w_ref, up_ref):
    steps = lax.broadcasted_iota(jnp.int32, (NT, NS), 0)

    def half(i, carry):
        e = 1 - i
        first = lax.rem(lax.axis_index("rcv") + 8 * e, 16) * NP + chunk * PC
        total = (p0[e].astype(F32) + p1[e].astype(F32)) + (p2[e].astype(F32) + p3[e].astype(F32))
        u = hi_lo_hi(total + r_ref[i].astype(F32), 0)
        acc = jnp.zeros((2 * ROWS, NS), F32)
        for j in range(PC):
            field = dot(a_ref[j], u)
            field = jnp.where(steps < on_ref[pl.ds(first + j, 1), :], field, 0.0).astype(BF)
            up_ref[j] = field
            acc += dot(t_ref[j], field)
        w_ref[e] = (acc[:ROWS] + acc[ROWS:]).astype(BF)
        return carry

    lax.fori_loop(0, 2, half, 0)


def flip_kernel(a_ref, b_ref, o_ref):
    for i, ref in enumerate((a_ref, b_ref)):
        for j in range(PC):
            o_ref[i * PC + j] = ref[j].T


def load_kernel(r_hbm, o_ref, sem):
    copies = [
        pltpu.make_async_copy(r_hbm.at[part, k], o_ref.at[part, k], sem.at[part, k])
        for k in range(NF)
        for part in range(2)
    ]
    for copy in copies:
        copy.start()
    for copy in copies:
        copy.wait()


def corr_kernel(w0, w1, w2, w3, v0, v1, v2, v3, r_ref, o0, o1, o2, o3, out, acc):
    x, zl, zh, y, c = place()
    refs = (w0, w1, w2, w3, v0, v1, v2, v3)
    row = lax.broadcasted_iota(jnp.int32, (256, NR), 0)
    even = row % 2 == 0

    def step(i, carry):
        for n in range(5):
            p = 5 * i + n
            t = (p >= 3).astype(jnp.int32) + (p >= 7).astype(jnp.int32)
            k = p - t
            at = pl.ds(pl.multiple_of(16 * t, 16), 16)
            m = jnp.concatenate([w[e, at] for w in refs for e in range(2)], axis=0)
            q = dot(m, r_ref[1, k])
            g = dot(m, r_ref[0, k]) + jnp.where(even, pltpu.roll(q, 255, 0), -pltpu.roll(q, 1, 0))
            mine = (row % 16 + 16 * t >= BIN * k) & (row % 16 + 16 * t < BIN * k + BIN)
            acc[t] = jnp.where(mine, g, acc[t])
        return carry

    lax.fori_loop(0, 2, step, 0)
    for i in range(16):
        other, d, e = i // 8, i // 2 % 4, i % 2
        yb = lax.rem(y + 4 - d, 4)
        xb = lax.rem(zh + e, 2) * 2 + yb // 2
        zb = lax.rem(yb, 2) * 2 + lax.rem(c + other, 2)
        out[lax.rem(xb + 4 - x, 4), zb ^ zl] = jnp.concatenate([acc[t, 16 * i : 16 * i + 16] for t in range(3)], axis=0).astype(BF)
    for d, ref in enumerate((o0, o1, o2, o3)):
        ref[...] = out[d]


def correlate(waves, reflection):
    return call(
        corr_kernel,
        [jax.ShapeDtypeStruct((4, ROWS, NR), BF)] * 4,
        "corr",
        in_specs=[pl.BlockSpec(memory_space=pltpu.VMEM)] * 9,
        scratch_shapes=[pltpu.VMEM((4, 4, ROWS, NR), BF), pltpu.VMEM((3, 256, NR), F32)],
        cost_estimate=cost(4),
        mib=16,
    )(*waves, reflection)


def sum_kernel(*refs):
    ins, (keep, *gives) = refs[: 4 * CH], refs[4 * CH :]
    for h in range(CH):
        g = ins[4 * h : 4 * h + 4]
        total = (g[0][...].astype(F32) + g[1][...].astype(F32)) + (g[2][...].astype(F32) + g[3][...].astype(F32))
        keep[h] = total[0]
        for d, give in enumerate(gives):
            give[h] = total[d + 1].astype(BF)


def refocus_kernel(g0, g1, g2, g3, d_ref, on_ref, a_ref, o_hbm, o_ref, sem):
    steps = lax.broadcasted_iota(jnp.int32, (NR, NT), 1)
    copies = []
    for h in range(CH):
        g = (g0[h] + g1[h].astype(F32)) + (g2[h].astype(F32) + g3[h].astype(F32))
        gt = hi_lo_hi(g.T, 1)
        for i in range(PC):
            j = h * PC + i
            field = dot(gt, a_ref[i], 1, 1)
            field = jnp.where(steps < on_ref[:, j : j + 1], field, 0.0)
            o_ref[j] = d_ref[j].astype(F32) + field
            copies.append(pltpu.make_async_copy(o_ref.at[j], o_hbm.at[j], sem.at[j]))
            copies[-1].start()
    for copy in copies:
        copy.wait()


def send(value, axis, to):
    return lax.ppermute(value, axis, [(i, to(i)) for i in range(16)])


def to_x(d):
    return lambda i: (i // 4 + d) % 4 * 4 + i % 4


def to_zl(d):
    return lambda i: i ^ d


def to_y(d):
    return lambda i: i // 8 * 8 + (i // 2 % 4 + d) % 4 * 2 + i % 2


def to_zh(i):
    return (i + 8) % 16


def to_core(i):
    return i ^ 1


def together(*lists):
    flat = lax.optimization_barrier(tuple(v for values in lists for v in values))
    out, at = [], 0
    for values in lists:
        out.append(list(flat[at : at + len(values)]))
        at += len(values)
    return out


def on_device(reflection, focusing, direct, onset_source, onset_receiver):
    t_spec = jnp.asarray(spectra_table())
    t_samp = jnp.asarray(samples_table())

    spectra = call(spectra_kernel, pltpu.VMEM((CH * ROWS, NR), BF), "spectra", mib=62,
        out_specs=pl.BlockSpec(memory_space=pltpu.VMEM),
        in_specs=[pl.BlockSpec(memory_space=pltpu.HBM)] * 2,
        scratch_shapes=[
            pltpu.VMEM((NP, NR, NT), BF),
            pltpu.VMEM((4 * NF, NT), BF),
            pltpu.SemaphoreType.DMA((NP + 1,)),
        ],
    )(
        focusing, jnp.asarray(trace_table())
    )
    near = [send(spectra, "src", to_zl(d)) for d in (1, 2, 3)]
    held = call(
        load_kernel,
        pltpu.VMEM((2, NF, NS, NR), BF),
        "load",
        in_specs=[pl.BlockSpec(memory_space=pltpu.HBM)],
        out_specs=pl.BlockSpec(memory_space=pltpu.VMEM),
        scratch_shapes=[pltpu.SemaphoreType.DMA((2, NF))],
        cost_estimate=cost(3),
        mib=50,
    )(reflection)
    near, [spectra, held] = together(near, [spectra, held])
    stack = jnp.stack([spectra, *near])
    pieces = [stack] + [send(stack, "src", to_x(d)) for d in (1, 2, 3)]

    def summed(give, keep):
        got = send(give, "rcv", to_core)
        return [(keep[d].astype(F32) + got[d].astype(F32)).astype(BF) for d in range(4)]

    def over_y(both):
        return [both[0]] + [send(both[d], "rcv", to_y(d)) for d in (1, 2, 3)]

    def half_sum(both):
        return ((both[0].astype(F32) + both[1].astype(F32)) + (both[2].astype(F32) + both[3].astype(F32))).astype(BF)

    def window(both, half, h):
        return call(
            functools.partial(window_kernel, h),
            (jax.ShapeDtypeStruct((2, ROWS, NS), BF), jax.ShapeDtypeStruct((PC, NT, NS), BF)),
            f"window{h}",
            cost_estimate=cost(2),
        )(*both, half, onset_source, t_samp, t_spec)

    sum_a = summed(*convolve(pieces, held, 0))
    both_a = over_y(sum_a)
    sum_b = summed(*convolve(pieces, held, 1))
    both_a[1:], sum_b = together(both_a[1:], sum_b)
    both_b = over_y(sum_b)
    half_a = send(half_sum(both_a), "rcv", to_zh)
    half_b = send(half_sum(both_b), "rcv", to_zh)
    [half_a], both_b = together([half_a], both_b)
    wave_a, field_a = window(both_a, half_a, 0)
    wave_b, field_b = window(both_b, half_b, 1)
    own_a = over_y([wave_a] * 4)
    own_b = over_y([wave_b] * 4)
    upgoing = call(
        flip_kernel, jax.ShapeDtypeStruct((NP, NS, NT), BF), "flip", cost_estimate=cost(2)
    )(field_a, field_b)
    parts = []
    own_a[:1], [upgoing] = together(own_a[:1], [upgoing])

    def over_core(own):
        return [*own, *[send(w, "rcv", to_core) for w in own]]

    def over_x(back):
        return [back[0]] + [send(back[d], "src", to_x(d)) for d in (1, 2, 3)]

    parts_a = over_x(correlate(over_core(own_a), held))
    own_b[1:3], parts_a[:1] = together(own_b[1:3], parts_a[:1])
    own_b[3:], parts_a[1:3] = together(own_b[3:], parts_a[1:3])
    parts = parts_a + over_x(correlate(over_core(own_b), held))

    keep, *gives = call(
        sum_kernel,
        [jax.ShapeDtypeStruct((CH, ROWS, NR), F32)] + [jax.ShapeDtypeStruct((CH, ROWS, NR), BF)] * 3,
        "sum_x",
    )(*parts)
    last = [keep] + [send(gives[d - 1], "src", to_zl(d)) for d in (1, 2, 3)]
    refocused = call(
        refocus_kernel,
        jax.ShapeDtypeStruct((NP, NR, NT), F32),
        "refocus",
        in_specs=[pl.BlockSpec(memory_space=pltpu.VMEM)] * 7,
        out_specs=pl.BlockSpec(memory_space=pltpu.HBM),
        scratch_shapes=[pltpu.VMEM((NP, NR, NT), F32), pltpu.SemaphoreType.DMA((NP,))],
    )(
        *last, direct, onset_receiver.T, t_samp
    )
    return (upgoing, refocused)


def solution(mesh):
    in_specs = (
        P(None, None, "src", "rcv"),
        P("src", "rcv", None),
        P("src", "rcv", None),
        P(None, "src"),
        P("src", "rcv"),
    )
    out_specs = (P("rcv", "src", None), P("src", "rcv", None))
    return jax.shard_map(
        on_device, mesh=mesh, in_specs=in_specs, out_specs=out_specs, check_vma=False
    )
```

```python
import functools
import math

import jax
import jax.numpy as jnp
import numpy as np
from jax import lax
from jax.experimental import pallas as pl
from jax.experimental.pallas import tpu as pltpu
from jax.sharding import PartitionSpec as P

NF = 8
NT = 128
NP = 6
PC = 3
CH = NP // PC
ROWS = 2 * NF * PC
BIN = 2 * PC
NS = 1024
NR = 256
BF = jnp.bfloat16
F32 = jnp.float32


def split(table):
    high = table.astype(BF)
    low = (table - high.astype(np.float32)).astype(BF)
    return high, low


def tables():
    k = np.arange(1, NF + 1)[:, None]
    t = np.arange(NT)[None, :]
    phase = 2.0 * math.pi / NT * ((k * t) % NT)
    return np.cos(phase).astype(np.float32), np.sin(phase).astype(np.float32)


def trace_table():
    cosines, sines = tables()
    return np.concatenate(split(np.stack([cosines, -sines], 1).reshape(2 * NF, NT)))


def spectra_table():
    cosines, sines = tables()
    full = np.zeros((PC, NF, PC, 2, NT), np.float32)
    for j in range(PC):
        full[j, :, j, 0] = cosines
        full[j, :, j, 1] = -sines
    return np.concatenate(split(full.reshape(PC, ROWS, NT)), axis=1)


def samples_table():
    cosines, sines = tables()
    full = np.zeros((PC, NT, NF, PC, 2), np.float32)
    for j in range(PC):
        full[j, :, :, j, 0] = 2.0 / NT * cosines.T
        full[j, :, :, j, 1] = -2.0 / NT * sines.T
    high, low = split(full.reshape(PC, NT, ROWS))
    return np.concatenate([high, high, low], axis=2)


def dot(a, b, ca=1, cb=0):
    return lax.dot_general(a, b, (((ca,), (cb,)), ((), ())), preferred_element_type=F32)


def hi_lo_hi(x, axis):
    high = x.astype(BF)
    low = (x - high.astype(F32)).astype(BF)
    return jnp.concatenate([high, low, high], axis=axis)


def place():
    src = lax.axis_index("src")
    rcv = lax.axis_index("rcv")
    return src // 4, src % 4, rcv // 8, (rcv // 2) % 4, rcv % 2


def call(kernel, out, name, mib=8, **kw):
    return pl.pallas_call(
        kernel,
        out_shape=out,
        name=name,
        compiler_params=pltpu.CompilerParams(vmem_limit_bytes=int(mib * 2**20)),
        **kw,
    )


def cost(us):
    return pl.CostEstimate(flops=int(us * 1e9), bytes_accessed=1 << 16, transcendentals=0)


def window_of(k, tile):
    low = BIN * k // tile * tile
    high = -(-BIN * (k + 1) // tile) * tile
    return low, high


def merge(parts, t, tile):
    bins = sorted({(8 * t) // BIN, (8 * t + 7) // BIN})
    out = None
    for k in bins:
        value = parts[k][..., 8 * t - window_of(k, tile)[0] :, :][..., :8, :]
        if out is None:
            out = value
        else:
            row = lax.broadcasted_iota(jnp.int32, value.shape, value.ndim - 2) + 8 * t
            out = jnp.where(row < BIN * k, out, value)
    return out


def spectra_kernel(f_hbm, t_hbm, o_ref, f_ref, t_ref, sem):
    copies = [pltpu.make_async_copy(f_hbm.at[j], f_ref.at[j], sem.at[j]) for j in range(NP)]
    copies.append(pltpu.make_async_copy(t_hbm, t_ref, sem.at[NP]))
    for copy in copies:
        copy.start()
    for copy in copies:
        copy.wait()
    rows = []
    for j in range(NP):
        both = dot(t_ref[...], f_ref[j], 1, 1)
        rows.append(both[: 2 * NF] + both[2 * NF :])
    r = lax.broadcasted_iota(jnp.int32, (CH * ROWS, CH * ROWS), 0)
    q = (r * 43) >> 8
    rest = r - BIN * q
    source = ((q >> 3) * PC + (rest >> 1)) * 16 + (q & 7) * 2 + (rest & 1)
    move = (lax.broadcasted_iota(jnp.int32, r.shape, 1) == source).astype(F32).astype(BF)
    o_ref[...] = dot(move, jnp.concatenate(rows, axis=0).astype(BF)).astype(BF)


def swap_rows(x):
    even = lax.broadcasted_iota(jnp.int32, x.shape, 0) % 2 == 0
    n = x.shape[0]
    return jnp.where(even, -pltpu.roll(x, n - 1, 0), pltpu.roll(x, 1, 0))


def conv_kernel(chunk, f0, f1, f2, f3, r_ref, give, keep, l1, l2):
    x, zl, zh, y, c = place()
    for dx, ref in ((0, f0), (2, f1), (1, f2), (3, f3)):
        for dz in range(4):
            xb = lax.rem(x + 4 - dx, 4)
            zb = zl ^ (3 - dz)
            yb = lax.rem(xb, 2) * 2 + zb // 2
            to = lax.rem(zb + c, 2) * 8 + lax.rem(yb + 4 - y, 4) * 2 + lax.rem(xb // 2 + zh, 2)
            rows = ref[dz, chunk * ROWS : (chunk + 1) * ROWS].astype(F32)
            l1[to] = rows
            l2[to] = swap_rows(rows)

    sb = 1024

    def step(i, carry):
        g, at = i, slice(None)
        parts = {}
        for k in range(4):
            low, high = window_of(k, 8)
            n = 16 * (high - low)
            rows = pl.ds(pl.multiple_of(g * 24, 8) + low, high - low)
            a1 = l1[:, rows].reshape(n, NR).astype(BF)
            a2 = l2[:, rows].reshape(n, NR).astype(BF)
            v = dot(a1, r_ref[0, 4 * g + k, at, :], 1, 1) + dot(a2, r_ref[1, 4 * g + k, at, :], 1, 1)
            parts[k] = v.reshape(16, high - low, sb)
        out = jnp.concatenate([merge(parts, t, 8) for t in range(3)], axis=1).astype(BF)
        keep[:, g, :, at] = out[:8]
        give[:, g, :, at] = out[8:]
        return carry

    lax.fori_loop(0, 2 * NS // sb, step, 0)


def convolve(pieces, reflection, chunk):
    give, keep = call(
        functools.partial(conv_kernel, chunk),
        [jax.ShapeDtypeStruct((8, 2, ROWS // 2, NS), BF)] * 2,
        f"conv{chunk}",
        in_specs=[pl.BlockSpec(memory_space=pltpu.VMEM)] * 5,
        scratch_shapes=[pltpu.VMEM((16, ROWS, NR), F32)] * 2,
        cost_estimate=cost(4),
    )(*pieces, reflection)
    return give.reshape(4, 2, ROWS, NS), keep.reshape(4, 2, ROWS, NS)


def window_kernel(chunk, p0, p1, p2, p3, r_ref, on_ref, a_ref, t_ref, w_ref, up_ref):
    steps = lax.broadcasted_iota(jnp.int32, (NT, NS), 0)

    def half(i, carry):
        e = 1 - i
        first = lax.rem(lax.axis_index("rcv") + 8 * e, 16) * NP + chunk * PC
        total = (p0[e].astype(F32) + p1[e].astype(F32)) + (p2[e].astype(F32) + p3[e].astype(F32))
        u = hi_lo_hi(total + r_ref[i].astype(F32), 0)
        acc = jnp.zeros((2 * ROWS, NS), F32)
        for j in range(PC):
            field = dot(a_ref[j], u)
            field = jnp.where(steps < on_ref[pl.ds(first + j, 1), :], field, 0.0).astype(BF)
            up_ref[j] = field
            acc += dot(t_ref[j], field)
        w_ref[e] = (acc[:ROWS] + acc[ROWS:]).astype(BF)
        return carry

    lax.fori_loop(0, 2, half, 0)


def flip_kernel(a_ref, b_ref, o_ref):
    for i, ref in enumerate((a_ref, b_ref)):
        for j in range(PC):
            o_ref[i * PC + j] = ref[j].T


def load_kernel(r_hbm, o_ref, sem):
    copies = [
        pltpu.make_async_copy(r_hbm.at[part, k], o_ref.at[part, k], sem.at[part, k])
        for k in range(NF)
        for part in range(2)
    ]
    for copy in copies:
        copy.start()
    for copy in copies:
        copy.wait()


def corr_kernel(w0, w1, w2, w3, v0, v1, v2, v3, r_ref, o0, o1, o2, o3, out, acc):
    x, zl, zh, y, c = place()
    refs = (w0, w1, w2, w3, v0, v1, v2, v3)
    row = lax.broadcasted_iota(jnp.int32, (256, NR), 0)
    even = row % 2 == 0

    def step(i, carry):
        for n in range(5):
            p = 5 * i + n
            t = (p >= 3).astype(jnp.int32) + (p >= 7).astype(jnp.int32)
            k = p - t
            at = pl.ds(pl.multiple_of(16 * t, 16), 16)
            m = jnp.concatenate([w[e, at] for w in refs for e in range(2)], axis=0)
            q = dot(m, r_ref[1, k])
            g = dot(m, r_ref[0, k]) + jnp.where(even, pltpu.roll(q, 255, 0), -pltpu.roll(q, 1, 0))
            mine = (row % 16 + 16 * t >= BIN * k) & (row % 16 + 16 * t < BIN * k + BIN)
            acc[t] = jnp.where(mine, g, acc[t])
        return carry

    lax.fori_loop(0, 2, step, 0)
    for i in range(16):
        other, d, e = i // 8, i // 2 % 4, i % 2
        yb = lax.rem(y + 4 - d, 4)
        xb = lax.rem(zh + e, 2) * 2 + yb // 2
        zb = lax.rem(yb, 2) * 2 + lax.rem(c + other, 2)
        out[lax.rem(xb + 4 - x, 4), zb ^ zl] = jnp.concatenate([acc[t, 16 * i : 16 * i + 16] for t in range(3)], axis=0).astype(BF)
    for d, ref in enumerate((o0, o1, o2, o3)):
        ref[...] = out[d]


def correlate(waves, reflection):
    return call(
        corr_kernel,
        [jax.ShapeDtypeStruct((4, ROWS, NR), BF)] * 4,
        "corr",
        in_specs=[pl.BlockSpec(memory_space=pltpu.VMEM)] * 9,
        scratch_shapes=[pltpu.VMEM((4, 4, ROWS, NR), BF), pltpu.VMEM((3, 256, NR), F32)],
        cost_estimate=cost(4),
        mib=16,
    )(*waves, reflection)


def sum_kernel(*refs):
    ins, (keep, *gives) = refs[: 4 * CH], refs[4 * CH :]
    for h in range(CH):
        g = ins[4 * h : 4 * h + 4]
        total = (g[0][...].astype(F32) + g[1][...].astype(F32)) + (g[2][...].astype(F32) + g[3][...].astype(F32))
        keep[h] = total[0]
        for d, give in enumerate(gives):
            give[h] = total[d + 1].astype(BF)


def refocus_kernel(g3, g2, g1, g0, d_ref, on_ref, a_ref, o_hbm, o_ref, sem):
    steps = lax.broadcasted_iota(jnp.int32, (NR, NT), 1)
    copies = []
    for h in range(CH):
        g = (g0[h] + g1[h].astype(F32)) + (g2[h].astype(F32) + g3[h].astype(F32))
        gt = hi_lo_hi(g.T, 1)
        for i in range(PC):
            j = h * PC + i
            field = dot(gt, a_ref[i], 1, 1)
            field = jnp.where(steps < on_ref[:, j : j + 1], field, 0.0)
            o_ref[j] = d_ref[j].astype(F32) + field
            copies.append(pltpu.make_async_copy(o_ref.at[j], o_hbm.at[j], sem.at[j]))
            copies[-1].start()
    for copy in copies:
        copy.wait()


def send(value, axis, to):
    return lax.ppermute(value, axis, [(i, to(i)) for i in range(16)])


def to_x(d):
    return lambda i: (i // 4 + d) % 4 * 4 + i % 4


def to_zl(d):
    return lambda i: i ^ d


def to_y(d):
    return lambda i: i // 8 * 8 + (i // 2 % 4 + d) % 4 * 2 + i % 2


def to_zh(i):
    return (i + 8) % 16


def to_core(i):
    return i ^ 1


def together(*lists):
    flat = lax.optimization_barrier(tuple(v for values in lists for v in values))
    out, at = [], 0
    for values in lists:
        out.append(list(flat[at : at + len(values)]))
        at += len(values)
    return out


def on_device(reflection, focusing, direct, onset_source, onset_receiver):
    t_spec = jnp.asarray(spectra_table())
    t_samp = jnp.asarray(samples_table())

    spectra = call(spectra_kernel, pltpu.VMEM((CH * ROWS, NR), BF), "spectra", mib=62,
        out_specs=pl.BlockSpec(memory_space=pltpu.VMEM),
        in_specs=[pl.BlockSpec(memory_space=pltpu.HBM)] * 2,
        scratch_shapes=[
            pltpu.VMEM((NP, NR, NT), BF),
            pltpu.VMEM((4 * NF, NT), BF),
            pltpu.SemaphoreType.DMA((NP + 1,)),
        ],
    )(
        focusing, jnp.asarray(trace_table())
    )
    near = [send(spectra, "src", to_zl(d)) for d in (3, 2, 1)]
    held = call(
        load_kernel,
        pltpu.VMEM((2, NF, NS, NR), BF),
        "load",
        in_specs=[pl.BlockSpec(memory_space=pltpu.HBM)],
        out_specs=pl.BlockSpec(memory_space=pltpu.VMEM),
        scratch_shapes=[pltpu.SemaphoreType.DMA((2, NF))],
        cost_estimate=cost(3),
        mib=50,
    )(reflection)
    near, [spectra, held] = together(near, [spectra, held])
    stack = jnp.stack([*near, spectra])
    pieces = [stack] + [send(stack, "src", to_x(d)) for d in (2, 1, 3)]

    def summed(give, keep):
        got = send(give, "rcv", to_core)
        return [(keep[d].astype(F32) + got[d].astype(F32)).astype(BF) for d in range(4)]

    def over_y(both):
        return [both[0]] + [send(both[d], "rcv", to_y(d)) for d in (1, 2, 3)]

    def half_sum(both):
        return ((both[0].astype(F32) + both[1].astype(F32)) + (both[2].astype(F32) + both[3].astype(F32))).astype(BF)

    def window(both, half, h):
        return call(
            functools.partial(window_kernel, h),
            (jax.ShapeDtypeStruct((2, ROWS, NS), BF), jax.ShapeDtypeStruct((PC, NT, NS), BF)),
            f"window{h}",
            cost_estimate=cost(2),
        )(*both, half, onset_source, t_samp, t_spec)

    sum_a = summed(*convolve(pieces, held, 0))
    both_a = over_y(sum_a)
    sum_b = summed(*convolve(pieces, held, 1))
    both_a[1:], sum_b = together(both_a[1:], sum_b)
    both_b = over_y(sum_b)
    half_a = send(half_sum(both_a), "rcv", to_zh)
    half_b = send(half_sum(both_b), "rcv", to_zh)
    [half_a], both_b = together([half_a], both_b)
    wave_a, field_a = window(both_a, half_a, 0)
    wave_b, field_b = window(both_b, half_b, 1)
    own_a = over_y([wave_a] * 4)
    own_b = over_y([wave_b] * 4)
    upgoing = call(
        flip_kernel, jax.ShapeDtypeStruct((NP, NS, NT), BF), "flip", cost_estimate=cost(2)
    )(field_a, field_b)
    parts = []
    own_a[:1], [upgoing] = together(own_a[:1], [upgoing])

    def over_core(own):
        return [*own, *[send(w, "rcv", to_core) for w in own]]

    def over_x(back):
        return [back[0]] + [send(back[d], "src", to_x(d)) for d in (2, 1, 3)]

    parts_a = over_x(correlate(over_core(own_a), held))
    own_b[1::2], parts_a[:1] = together(own_b[1::2], parts_a[:1])
    own_b[2:3], parts_a[1:3] = together(own_b[2:3], parts_a[1:3])
    parts = parts_a + over_x(correlate(over_core(own_b), held))

    keep, *gives = call(
        sum_kernel,
        [jax.ShapeDtypeStruct((CH, ROWS, NR), F32)] + [jax.ShapeDtypeStruct((CH, ROWS, NR), BF)] * 3,
        "sum_x",
    )(*parts)
    last = [send(gives[d - 1], "src", to_zl(d)) for d in (3, 2, 1)]
    refocused = call(
        refocus_kernel,
        jax.ShapeDtypeStruct((NP, NR, NT), F32),
        "refocus",
        in_specs=[pl.BlockSpec(memory_space=pltpu.VMEM)] * 7,
        out_specs=pl.BlockSpec(memory_space=pltpu.HBM),
        scratch_shapes=[pltpu.VMEM((NP, NR, NT), F32), pltpu.SemaphoreType.DMA((NP,))],
    )(
        *last, keep, direct, onset_receiver.T, t_samp
    )
    return (upgoing, refocused)


def solution(mesh):
    in_specs = (
        P(None, None, "src", "rcv"),
        P("src", "rcv", None),
        P("src", "rcv", None),
        P(None, "src"),
        P("src", "rcv"),
    )
    out_specs = (P("rcv", "src", None), P("src", "rcv", None))
    return jax.shard_map(
        on_device, mesh=mesh, in_specs=in_specs, out_specs=out_specs, check_vma=False
    )
```

```python
import functools
import math

import jax
import jax.numpy as jnp
import numpy as np
from jax import lax
from jax.experimental import pallas as pl
from jax.experimental.pallas import tpu as pltpu
from jax.sharding import PartitionSpec as P

NF = 8
NT = 128
NP = 6
PC = 3
CH = NP // PC
ROWS = 2 * NF * PC
BIN = 2 * PC
NS = 1024
NR = 256
BF = jnp.bfloat16
F32 = jnp.float32


def split(table):
    high = table.astype(BF)
    low = (table - high.astype(np.float32)).astype(BF)
    return high, low


def tables():
    k = np.arange(1, NF + 1)[:, None]
    t = np.arange(NT)[None, :]
    phase = 2.0 * math.pi / NT * ((k * t) % NT)
    return np.cos(phase).astype(np.float32), np.sin(phase).astype(np.float32)


def trace_table():
    cosines, sines = tables()
    return np.concatenate(split(np.stack([cosines, -sines], 1).reshape(2 * NF, NT)))


def spectra_table():
    cosines, sines = tables()
    full = np.zeros((PC, NF, PC, 2, NT), np.float32)
    for j in range(PC):
        full[j, :, j, 0] = cosines
        full[j, :, j, 1] = -sines
    return np.concatenate(split(full.reshape(PC, ROWS, NT)), axis=1)


def samples_table():
    cosines, sines = tables()
    full = np.zeros((PC, NT, NF, PC, 2), np.float32)
    for j in range(PC):
        full[j, :, :, j, 0] = 2.0 / NT * cosines.T
        full[j, :, :, j, 1] = -2.0 / NT * sines.T
    high, low = split(full.reshape(PC, NT, ROWS))
    return np.concatenate([high, high, low], axis=2)


def dot(a, b, ca=1, cb=0):
    return lax.dot_general(a, b, (((ca,), (cb,)), ((), ())), preferred_element_type=F32)


def hi_lo_hi(x, axis):
    high = x.astype(BF)
    low = (x - high.astype(F32)).astype(BF)
    return jnp.concatenate([high, low, high], axis=axis)


def place():
    src = lax.axis_index("src")
    rcv = lax.axis_index("rcv")
    return src // 4, src % 4, rcv // 8, (rcv // 2) % 4, rcv % 2


def call(kernel, out, name, mib=8, **kw):
    return pl.pallas_call(
        kernel,
        out_shape=out,
        name=name,
        compiler_params=pltpu.CompilerParams(vmem_limit_bytes=int(mib * 2**20)),
        **kw,
    )


def cost(us):
    return pl.CostEstimate(flops=int(us * 1e9), bytes_accessed=1 << 16, transcendentals=0)


def window_of(k, tile):
    low = BIN * k // tile * tile
    high = -(-BIN * (k + 1) // tile) * tile
    return low, high


def merge(parts, t, tile):
    bins = sorted({(8 * t) // BIN, (8 * t + 7) // BIN})
    out = None
    for k in bins:
        value = parts[k][..., 8 * t - window_of(k, tile)[0] :, :][..., :8, :]
        if out is None:
            out = value
        else:
            row = lax.broadcasted_iota(jnp.int32, value.shape, value.ndim - 2) + 8 * t
            out = jnp.where(row < BIN * k, out, value)
    return out


def spectra_kernel(f_hbm, t_hbm, o_ref, f_ref, t_ref, sem):
    copies = [pltpu.make_async_copy(f_hbm.at[j], f_ref.at[j], sem.at[j]) for j in range(NP)]
    copies.append(pltpu.make_async_copy(t_hbm, t_ref, sem.at[NP]))
    for copy in copies:
        copy.start()
    for copy in copies:
        copy.wait()
    rows = []
    for j in range(NP):
        both = dot(t_ref[...], f_ref[j], 1, 1)
        rows.append(both[: 2 * NF] + both[2 * NF :])
    r = lax.broadcasted_iota(jnp.int32, (CH * ROWS, CH * ROWS), 0)
    q = (r * 43) >> 8
    rest = r - BIN * q
    source = ((q >> 3) * PC + (rest >> 1)) * 16 + (q & 7) * 2 + (rest & 1)
    move = (lax.broadcasted_iota(jnp.int32, r.shape, 1) == source).astype(F32).astype(BF)
    o_ref[...] = dot(move, jnp.concatenate(rows, axis=0).astype(BF)).astype(BF)


def swap_rows(x):
    even = lax.broadcasted_iota(jnp.int32, x.shape, 0) % 2 == 0
    n = x.shape[0]
    return jnp.where(even, -pltpu.roll(x, n - 1, 0), pltpu.roll(x, 1, 0))


def conv_kernel(chunk, f0, f1, f2, f3, r_ref, give, keep, l1, l2):
    x, zl, zh, y, c = place()
    for dx, ref in ((0, f0), (2, f1), (1, f2), (3, f3)):
        for dz in range(4):
            xb = lax.rem(x + 4 - dx, 4)
            zb = zl ^ (3 - dz)
            yb = lax.rem(xb, 2) * 2 + zb // 2
            to = lax.rem(zb + c, 2) * 8 + lax.rem(yb + 4 - y, 4) * 2 + lax.rem(xb // 2 + zh, 2)
            rows = ref[dz, chunk * ROWS : (chunk + 1) * ROWS].astype(F32)
            l1[to] = rows
            l2[to] = swap_rows(rows)

    sb = 1024

    def step(i, carry):
        g, at = i, slice(None)
        parts = {}
        for k in range(4):
            low, high = window_of(k, 8)
            n = 16 * (high - low)
            rows = pl.ds(pl.multiple_of(g * 24, 8) + low, high - low)
            a1 = l1[:, rows].reshape(n, NR).astype(BF)
            a2 = l2[:, rows].reshape(n, NR).astype(BF)
            v = dot(a1, r_ref[0, 4 * g + k, at, :], 1, 1) + dot(a2, r_ref[1, 4 * g + k, at, :], 1, 1)
            parts[k] = v.reshape(16, high - low, sb)
        out = jnp.concatenate([merge(parts, t, 8) for t in range(3)], axis=1).astype(BF)
        keep[:, g, :, at] = out[:8]
        give[:, g, :, at] = out[8:]
        return carry

    lax.fori_loop(0, 2 * NS // sb, step, 0)


def convolve(pieces, reflection, chunk):
    give, keep = call(
        functools.partial(conv_kernel, chunk),
        [jax.ShapeDtypeStruct((8, 2, ROWS // 2, NS), BF)] * 2,
        f"conv{chunk}",
        in_specs=[pl.BlockSpec(memory_space=pltpu.VMEM)] * 5,
        scratch_shapes=[pltpu.VMEM((16, ROWS, NR), F32)] * 2,
        cost_estimate=cost(4),
    )(*pieces, reflection)
    return give.reshape(4, 2, ROWS, NS), keep.reshape(4, 2, ROWS, NS)


def window_kernel(chunk, p0, p1, p2, p3, r_ref, on_ref, a_ref, t_ref, w_ref, up_ref):
    steps = lax.broadcasted_iota(jnp.int32, (NT, NS), 0)

    def half(i, carry):
        e = 1 - i
        first = lax.rem(lax.axis_index("rcv") + 8 * e, 16) * NP + chunk * PC
        total = (p0[e].astype(F32) + p1[e].astype(F32)) + (p2[e].astype(F32) + p3[e].astype(F32))
        u = hi_lo_hi(total + r_ref[i].astype(F32), 0)
        acc = jnp.zeros((2 * ROWS, NS), F32)
        for j in range(PC):
            field = dot(a_ref[j], u)
            field = jnp.where(steps < on_ref[pl.ds(first + j, 1), :], field, 0.0).astype(BF)
            up_ref[j] = field
            acc += dot(t_ref[j], field)
        w_ref[e] = (acc[:ROWS] + acc[ROWS:]).astype(BF)
        return carry

    lax.fori_loop(0, 2, half, 0)


def flip_kernel(a_ref, b_ref, o_ref):
    for i, ref in enumerate((a_ref, b_ref)):
        for j in range(PC):
            o_ref[i * PC + j] = ref[j].T


def load_kernel(r_hbm, o_ref, sem):
    copies = [
        pltpu.make_async_copy(r_hbm.at[part, k], o_ref.at[part, k], sem.at[part, k])
        for k in range(NF)
        for part in range(2)
    ]
    for copy in copies:
        copy.start()
    for copy in copies:
        copy.wait()


def corr_kernel(w0, w1, w2, w3, v0, v1, v2, v3, r_ref, o0, o1, o2, o3, out, acc):
    x, zl, zh, y, c = place()
    refs = (w0, w1, w2, w3, v0, v1, v2, v3)
    row = lax.broadcasted_iota(jnp.int32, (256, NR), 0)
    even = row % 2 == 0

    def step(i, carry):
        for n in range(5):
            p = 5 * i + n
            t = (p >= 3).astype(jnp.int32) + (p >= 7).astype(jnp.int32)
            k = p - t
            at = pl.ds(pl.multiple_of(16 * t, 16), 16)
            m = jnp.concatenate([w[e, at] for w in refs for e in range(2)], axis=0)
            q = dot(m, r_ref[1, k])
            g = dot(m, r_ref[0, k]) + jnp.where(even, pltpu.roll(q, 255, 0), -pltpu.roll(q, 1, 0))
            mine = (row % 16 + 16 * t >= BIN * k) & (row % 16 + 16 * t < BIN * k + BIN)
            acc[t] = jnp.where(mine, g, acc[t])
        return carry

    lax.fori_loop(0, 2, step, 0)
    for i in range(16):
        other, d, e = i // 8, (0, 2, 1, 3)[i // 2 % 4], i % 2
        yb = lax.rem(y + 4 - d, 4)
        xb = lax.rem(zh + e, 2) * 2 + yb // 2
        zb = lax.rem(yb, 2) * 2 + lax.rem(c + other, 2)
        out[lax.rem(xb + 4 - x, 4), zb ^ zl] = jnp.concatenate([acc[t, 16 * i : 16 * i + 16] for t in range(3)], axis=0).astype(BF)
    for d, ref in enumerate((o0, o1, o2, o3)):
        ref[...] = out[d]


def correlate(waves, reflection):
    return call(
        corr_kernel,
        [jax.ShapeDtypeStruct((4, ROWS, NR), BF)] * 4,
        "corr",
        in_specs=[pl.BlockSpec(memory_space=pltpu.VMEM)] * 9,
        scratch_shapes=[pltpu.VMEM((4, 4, ROWS, NR), BF), pltpu.VMEM((3, 256, NR), F32)],
        cost_estimate=cost(4),
        mib=16,
    )(*waves, reflection)


def sum_kernel(*refs):
    ins, (keep, *gives) = refs[: 4 * CH], refs[4 * CH :]
    for h in range(CH):
        g = ins[4 * h : 4 * h + 4]
        total = (g[0][...].astype(F32) + g[1][...].astype(F32)) + (g[2][...].astype(F32) + g[3][...].astype(F32))
        keep[h] = total[0]
        for d, give in enumerate(gives):
            give[h] = total[d + 1].astype(BF)


def refocus_kernel(g3, g2, g1, g0, d_ref, on_ref, a_ref, o_hbm, o_ref, sem):
    steps = lax.broadcasted_iota(jnp.int32, (NR, NT), 1)
    copies = []
    for h in range(CH):
        g = (g0[h] + g1[h].astype(F32)) + (g2[h].astype(F32) + g3[h].astype(F32))
        gt = hi_lo_hi(g.T, 1)
        for i in range(PC):
            j = h * PC + i
            field = dot(gt, a_ref[i], 1, 1)
            field = jnp.where(steps < on_ref[:, j : j + 1], field, 0.0)
            o_ref[j] = d_ref[j].astype(F32) + field
            copies.append(pltpu.make_async_copy(o_ref.at[j], o_hbm.at[j], sem.at[j]))
            copies[-1].start()
    for copy in copies:
        copy.wait()


def send(value, axis, to):
    return lax.ppermute(value, axis, [(i, to(i)) for i in range(16)])


def to_x(d):
    return lambda i: (i // 4 + d) % 4 * 4 + i % 4


def to_zl(d):
    return lambda i: i ^ d


def to_y(d):
    return lambda i: i // 8 * 8 + (i // 2 % 4 + d) % 4 * 2 + i % 2


def to_zh(i):
    return (i + 8) % 16


def to_core(i):
    return i ^ 1


def together(*lists):
    flat = lax.optimization_barrier(tuple(v for values in lists for v in values))
    out, at = [], 0
    for values in lists:
        out.append(list(flat[at : at + len(values)]))
        at += len(values)
    return out


def on_device(reflection, focusing, direct, onset_source, onset_receiver):
    t_spec = jnp.asarray(spectra_table())
    t_samp = jnp.asarray(samples_table())

    spectra = call(spectra_kernel, pltpu.VMEM((CH * ROWS, NR), BF), "spectra", mib=62,
        out_specs=pl.BlockSpec(memory_space=pltpu.VMEM),
        in_specs=[pl.BlockSpec(memory_space=pltpu.HBM)] * 2,
        scratch_shapes=[
            pltpu.VMEM((NP, NR, NT), BF),
            pltpu.VMEM((4 * NF, NT), BF),
            pltpu.SemaphoreType.DMA((NP + 1,)),
        ],
    )(
        focusing, jnp.asarray(trace_table())
    )
    near = [send(spectra, "src", to_zl(d)) for d in (3, 2, 1)]
    held = call(
        load_kernel,
        pltpu.VMEM((2, NF, NS, NR), BF),
        "load",
        in_specs=[pl.BlockSpec(memory_space=pltpu.HBM)],
        out_specs=pl.BlockSpec(memory_space=pltpu.VMEM),
        scratch_shapes=[pltpu.SemaphoreType.DMA((2, NF))],
        cost_estimate=cost(3),
        mib=50,
    )(reflection)
    near, [spectra, held] = together(near, [spectra, held])
    stack = jnp.stack([*near, spectra])
    pieces = [stack] + [send(stack, "src", to_x(d)) for d in (2, 1, 3)]

    def summed(give, keep):
        got = send(give, "rcv", to_core)
        return [(keep[d].astype(F32) + got[d].astype(F32)).astype(BF) for d in range(4)]

    def over_y(both):
        return [both[0]] + [send(both[d], "rcv", to_y(d)) for d in (2, 1, 3)]

    def half_sum(both):
        return ((both[0].astype(F32) + both[1].astype(F32)) + (both[2].astype(F32) + both[3].astype(F32))).astype(BF)

    def window(both, half, h):
        return call(
            functools.partial(window_kernel, h),
            (jax.ShapeDtypeStruct((2, ROWS, NS), BF), jax.ShapeDtypeStruct((PC, NT, NS), BF)),
            f"window{h}",
            cost_estimate=cost(2),
        )(*both, half, onset_source, t_samp, t_spec)

    sum_a = summed(*convolve(pieces, held, 0))
    both_a = over_y(sum_a)
    sum_b = summed(*convolve(pieces, held, 1))
    both_a[1:], sum_b = together(both_a[1:], sum_b)
    both_b = over_y(sum_b)
    half_a = send(half_sum(both_a), "rcv", to_zh)
    half_b = send(half_sum(both_b), "rcv", to_zh)
    [half_a], both_b = together([half_a], both_b)
    wave_a, field_a = window(both_a, half_a, 0)
    wave_b, field_b = window(both_b, half_b, 1)
    own_a = over_y([wave_a] * 4)
    own_b = over_y([wave_b] * 4)
    upgoing = call(
        flip_kernel, jax.ShapeDtypeStruct((NP, NS, NT), BF), "flip", cost_estimate=cost(2)
    )(field_a, field_b)
    parts = []
    own_a[:1], [upgoing] = together(own_a[:1], [upgoing])

    def over_core(own):
        return [*own, *[send(w, "rcv", to_core) for w in own]]

    def over_x(back):
        return [back[0]] + [send(back[d], "src", to_x(d)) for d in (2, 1, 3)]

    parts_a = over_x(correlate(over_core(own_a), held))
    own_b[2:], parts_a[:1] = together(own_b[2:], parts_a[:1])
    own_b[1:2], parts_a[2:3] = together(own_b[1:2], parts_a[2:3])
    parts = parts_a + over_x(correlate(over_core(own_b), held))

    keep, *gives = call(
        sum_kernel,
        [jax.ShapeDtypeStruct((CH, ROWS, NR), F32)] + [jax.ShapeDtypeStruct((CH, ROWS, NR), BF)] * 3,
        "sum_x",
    )(*parts)
    last = [send(gives[d - 1], "src", to_zl(d)) for d in (3, 2, 1)]
    refocused = call(
        refocus_kernel,
        jax.ShapeDtypeStruct((NP, NR, NT), F32),
        "refocus",
        in_specs=[pl.BlockSpec(memory_space=pltpu.VMEM)] * 7,
        out_specs=pl.BlockSpec(memory_space=pltpu.HBM),
        scratch_shapes=[pltpu.VMEM((NP, NR, NT), F32), pltpu.SemaphoreType.DMA((NP,))],
    )(
        *last, keep, direct, onset_receiver.T, t_samp
    )
    return (upgoing, refocused)


def solution(mesh):
    in_specs = (
        P(None, None, "src", "rcv"),
        P("src", "rcv", None),
        P("src", "rcv", None),
        P(None, "src"),
        P("src", "rcv"),
    )
    out_specs = (P("rcv", "src", None), P("src", "rcv", None))
    return jax.shard_map(
        on_device, mesh=mesh, in_specs=in_specs, out_specs=out_specs, check_vma=False
    )
```

```python
import functools
import math

import jax
import jax.numpy as jnp
import numpy as np
from jax import lax
from jax.experimental import pallas as pl
from jax.experimental.pallas import tpu as pltpu
from jax.sharding import PartitionSpec as P

NF = 8
NT = 128
NP = 6
PC = 3
CH = NP // PC
ROWS = 2 * NF * PC
BIN = 2 * PC
NS = 1024
NR = 256
BF = jnp.bfloat16
F32 = jnp.float32


def split(table):
    high = table.astype(BF)
    low = (table - high.astype(np.float32)).astype(BF)
    return high, low


def tables():
    k = np.arange(1, NF + 1)[:, None]
    t = np.arange(NT)[None, :]
    phase = 2.0 * math.pi / NT * ((k * t) % NT)
    return np.cos(phase).astype(np.float32), np.sin(phase).astype(np.float32)


def trace_table():
    cosines, sines = tables()
    return np.concatenate(split(np.stack([cosines, -sines], 1).reshape(2 * NF, NT)))


def spectra_table():
    cosines, sines = tables()
    full = np.zeros((PC, NF, PC, 2, NT), np.float32)
    for j in range(PC):
        full[j, :, j, 0] = cosines
        full[j, :, j, 1] = -sines
    return np.concatenate(split(full.reshape(PC, ROWS, NT)), axis=1)


def samples_table():
    cosines, sines = tables()
    full = np.zeros((PC, NT, NF, PC, 2), np.float32)
    for j in range(PC):
        full[j, :, :, j, 0] = 2.0 / NT * cosines.T
        full[j, :, :, j, 1] = -2.0 / NT * sines.T
    high, low = split(full.reshape(PC, NT, ROWS))
    return np.concatenate([high, high, low], axis=2)


def dot(a, b, ca=1, cb=0):
    return lax.dot_general(a, b, (((ca,), (cb,)), ((), ())), preferred_element_type=F32)


def hi_lo_hi(x, axis):
    high = x.astype(BF)
    low = (x - high.astype(F32)).astype(BF)
    return jnp.concatenate([high, low, high], axis=axis)


def place():
    src = lax.axis_index("src")
    rcv = lax.axis_index("rcv")
    return src // 4, src % 4, rcv // 8, (rcv // 2) % 4, rcv % 2


def call(kernel, out, name, mib=8, **kw):
    return pl.pallas_call(
        kernel,
        out_shape=out,
        name=name,
        compiler_params=pltpu.CompilerParams(vmem_limit_bytes=int(mib * 2**20)),
        **kw,
    )


def cost(us):
    return pl.CostEstimate(flops=int(us * 1e9), bytes_accessed=1 << 16, transcendentals=0)


def window_of(k, tile):
    low = BIN * k // tile * tile
    high = -(-BIN * (k + 1) // tile) * tile
    return low, high


def merge(parts, t, tile):
    bins = sorted({(8 * t) // BIN, (8 * t + 7) // BIN})
    out = None
    for k in bins:
        value = parts[k][..., 8 * t - window_of(k, tile)[0] :, :][..., :8, :]
        if out is None:
            out = value
        else:
            row = lax.broadcasted_iota(jnp.int32, value.shape, value.ndim - 2) + 8 * t
            out = jnp.where(row < BIN * k, out, value)
    return out


def spectra_kernel(f_hbm, t_hbm, o_ref, f_ref, t_ref, sem):
    copies = [pltpu.make_async_copy(f_hbm.at[j], f_ref.at[j], sem.at[j]) for j in range(NP)]
    copies.append(pltpu.make_async_copy(t_hbm, t_ref, sem.at[NP]))
    for copy in copies:
        copy.start()
    for copy in copies:
        copy.wait()
    rows = []
    for j in range(NP):
        both = dot(t_ref[...], f_ref[j], 1, 1)
        rows.append(both[: 2 * NF] + both[2 * NF :])
    r = lax.broadcasted_iota(jnp.int32, (CH * ROWS, CH * ROWS), 0)
    q = (r * 43) >> 8
    rest = r - BIN * q
    source = ((q >> 3) * PC + (rest >> 1)) * 16 + (q & 7) * 2 + (rest & 1)
    move = (lax.broadcasted_iota(jnp.int32, r.shape, 1) == source).astype(F32).astype(BF)
    o_ref[...] = dot(move, jnp.concatenate(rows, axis=0).astype(BF)).astype(BF)


def swap_rows(x):
    even = lax.broadcasted_iota(jnp.int32, x.shape, 0) % 2 == 0
    n = x.shape[0]
    return jnp.where(even, -pltpu.roll(x, n - 1, 0), pltpu.roll(x, 1, 0))


def conv_kernel(chunk, f0, f1, f2, f3, r_ref, give, keep, l1, l2):
    x, zl, zh, y, c = place()
    for dx, ref in ((0, f0), (2, f1), (1, f2), (3, f3)):
        for dz in range(4):
            xb = lax.rem(x + 4 - dx, 4)
            zb = zl ^ (3 - dz)
            yb = lax.rem(xb, 2) * 2 + zb // 2
            to = lax.rem(zb + c, 2) * 8 + lax.rem(yb + 4 - y, 4) * 2 + lax.rem(xb // 2 + zh, 2)
            rows = ref[dz, chunk * ROWS : (chunk + 1) * ROWS].astype(F32)
            l1[to] = rows
            l2[to] = swap_rows(rows)

    sb = 1024

    def step(i, carry):
        g, at = i, slice(None)
        parts = {}
        for k in range(4):
            low, high = window_of(k, 8)
            n = 16 * (high - low)
            rows = pl.ds(pl.multiple_of(g * 24, 8) + low, high - low)
            a1 = l1[:, rows].reshape(n, NR).astype(BF)
            a2 = l2[:, rows].reshape(n, NR).astype(BF)
            v = dot(a1, r_ref[0, 4 * g + k, at, :], 1, 1) + dot(a2, r_ref[1, 4 * g + k, at, :], 1, 1)
            parts[k] = v.reshape(16, high - low, sb)
        out = jnp.concatenate([merge(parts, t, 8) for t in range(3)], axis=1).astype(BF)
        keep[:, g, :, at] = out[:8]
        give[:, g, :, at] = out[8:]
        return carry

    lax.fori_loop(0, 2 * NS // sb, step, 0)


def convolve(pieces, reflection, chunk):
    give, keep = call(
        functools.partial(conv_kernel, chunk),
        [jax.ShapeDtypeStruct((8, 2, ROWS // 2, NS), BF)] * 2,
        f"conv{chunk}",
        in_specs=[pl.BlockSpec(memory_space=pltpu.VMEM)] * 5,
        scratch_shapes=[pltpu.VMEM((16, ROWS, NR), F32)] * 2,
        cost_estimate=cost(4),
    )(*pieces, reflection)
    return give.reshape(4, 2, ROWS, NS), keep.reshape(4, 2, ROWS, NS)


def window_kernel(chunk, p0, p1, p2, p3, r_ref, on_ref, a_ref, t_ref, w_ref, up_ref):
    steps = lax.broadcasted_iota(jnp.int32, (NT, NS), 0)

    def half(i, carry):
        e = 1 - i
        first = lax.rem(lax.axis_index("rcv") + 8 * e, 16) * NP + chunk * PC
        total = (p0[e].astype(F32) + p1[e].astype(F32)) + (p2[e].astype(F32) + p3[e].astype(F32))
        u = hi_lo_hi(total + r_ref[i].astype(F32), 0)
        acc = jnp.zeros((2 * ROWS, NS), F32)
        for j in range(PC):
            field = dot(a_ref[j], u)
            field = jnp.where(steps < on_ref[pl.ds(first + j, 1), :], field, 0.0).astype(BF)
            up_ref[j] = field
            acc += dot(t_ref[j], field)
        w_ref[e] = (acc[:ROWS] + acc[ROWS:]).astype(BF)
        return carry

    lax.fori_loop(0, 2, half, 0)


def flip_kernel(a_ref, b_ref, o_ref):
    for i, ref in enumerate((a_ref, b_ref)):
        for j in range(PC):
            o_ref[i * PC + j] = ref[j].T


def load_kernel(r_hbm, o_ref, sem):
    copies = [
        pltpu.make_async_copy(r_hbm.at[part, k], o_ref.at[part, k], sem.at[part, k])
        for k in range(NF)
        for part in range(2)
    ]
    for copy in copies:
        copy.start()
    for copy in copies:
        copy.wait()


def corr_kernel(w0, w1, w2, w3, v0, v1, v2, v3, r_ref, o0, o1, o2, o3, out, acc):
    x, zl, zh, y, c = place()
    refs = (w0, w1, w2, w3, v0, v1, v2, v3)
    row = lax.broadcasted_iota(jnp.int32, (256, NR), 0)
    even = row % 2 == 0

    def step(i, carry):
        for n in range(5):
            p = 5 * i + n
            t = (p >= 3).astype(jnp.int32) + (p >= 7).astype(jnp.int32)
            k = p - t
            at = pl.ds(pl.multiple_of(16 * t, 16), 16)
            m = jnp.concatenate([w[e, at] for w in refs for e in range(2)], axis=0)
            q = dot(m, r_ref[1, k])
            g = dot(m, r_ref[0, k]) + jnp.where(even, pltpu.roll(q, 255, 0), -pltpu.roll(q, 1, 0))
            mine = (row % 16 + 16 * t >= BIN * k) & (row % 16 + 16 * t < BIN * k + BIN)
            acc[t] = jnp.where(mine, g, acc[t])
        return carry

    lax.fori_loop(0, 2, step, 0)
    for i in range(16):
        other, d, e = i // 8, (0, 2, 1, 3)[i // 2 % 4], i % 2
        yb = lax.rem(y + 4 - d, 4)
        xb = lax.rem(zh + e, 2) * 2 + yb // 2
        zb = lax.rem(yb, 2) * 2 + lax.rem(c + other, 2)
        out[lax.rem(xb + 4 - x, 4), zb ^ zl] = jnp.concatenate([acc[t, 16 * i : 16 * i + 16] for t in range(3)], axis=0).astype(BF)
    for d, ref in enumerate((o0, o1, o2, o3)):
        ref[...] = out[d]


def correlate(waves, reflection):
    return call(
        corr_kernel,
        [jax.ShapeDtypeStruct((4, ROWS, NR), BF)] * 4,
        "corr",
        in_specs=[pl.BlockSpec(memory_space=pltpu.VMEM)] * 9,
        scratch_shapes=[pltpu.VMEM((4, 4, ROWS, NR), BF), pltpu.VMEM((3, 256, NR), F32)],
        cost_estimate=cost(4),
        mib=16,
    )(*waves, reflection)


def sum_kernel(*refs):
    ins, (keep, *gives) = refs[: 4 * CH], refs[4 * CH :]
    for h in range(CH):
        g = ins[4 * h : 4 * h + 4]
        total = (g[0][...].astype(F32) + g[1][...].astype(F32)) + (g[2][...].astype(F32) + g[3][...].astype(F32))
        keep[h] = total[0]
        for d, give in enumerate(gives):
            give[h] = total[d + 1].astype(BF)


def refocus_kernel(g3, g2, g1, g0, d_ref, on_ref, a_ref, o_hbm, o_ref, sem):
    steps = lax.broadcasted_iota(jnp.int32, (NR, NT), 1)
    copies = []
    for h in range(CH):
        g = (g0[h] + g1[h].astype(F32)) + (g2[h].astype(F32) + g3[h].astype(F32))
        gt = hi_lo_hi(g.T, 1)
        for i in range(PC):
            j = h * PC + i
            field = dot(gt, a_ref[i], 1, 1)
            field = jnp.where(steps < on_ref[:, j : j + 1], field, 0.0)
            o_ref[j] = d_ref[j].astype(F32) + field
            copies.append(pltpu.make_async_copy(o_ref.at[j], o_hbm.at[j], sem.at[j]))
            copies[-1].start()
    for copy in copies:
        copy.wait()


def send(value, axis, to):
    return lax.ppermute(value, axis, [(i, to(i)) for i in range(16)])


def to_x(d):
    return lambda i: (i // 4 + d) % 4 * 4 + i % 4


def to_zl(d):
    return lambda i: i ^ d


def to_y(d):
    return lambda i: i // 8 * 8 + (i // 2 % 4 + d) % 4 * 2 + i % 2


def to_zh(i):
    return (i + 8) % 16


def to_core(i):
    return i ^ 1


def together(*lists):
    flat = lax.optimization_barrier(tuple(v for values in lists for v in values))
    out, at = [], 0
    for values in lists:
        out.append(list(flat[at : at + len(values)]))
        at += len(values)
    return out


def on_device(reflection, focusing, direct, onset_source, onset_receiver):
    t_spec = jnp.asarray(spectra_table())
    t_samp = jnp.asarray(samples_table())

    spectra = call(spectra_kernel, pltpu.VMEM((CH * ROWS, NR), BF), "spectra", mib=62,
        out_specs=pl.BlockSpec(memory_space=pltpu.VMEM),
        in_specs=[pl.BlockSpec(memory_space=pltpu.HBM)] * 2,
        scratch_shapes=[
            pltpu.VMEM((NP, NR, NT), BF),
            pltpu.VMEM((4 * NF, NT), BF),
            pltpu.SemaphoreType.DMA((NP + 1,)),
        ],
    )(
        focusing, jnp.asarray(trace_table())
    )
    near = [send(spectra, "src", to_zl(d)) for d in (3, 2, 1)]
    stack = jnp.stack([*near, spectra])
    [reflection], [stack] = together([reflection], [stack])
    pieces = [stack] + [send(stack, "src", to_x(d)) for d in (2, 1, 3)]

    held = call(
        load_kernel,
        pltpu.VMEM((2, NF, NS, NR), BF),
        "load",
        in_specs=[pl.BlockSpec(memory_space=pltpu.HBM)],
        out_specs=pl.BlockSpec(memory_space=pltpu.VMEM),
        scratch_shapes=[pltpu.SemaphoreType.DMA((2, NF))],
        cost_estimate=cost(3),
        mib=50,
    )(reflection)
    def summed(give, keep):
        got = send(give, "rcv", to_core)
        return [(keep[d].astype(F32) + got[d].astype(F32)).astype(BF) for d in range(4)]

    def over_y(both):
        return [both[0]] + [send(both[d], "rcv", to_y(d)) for d in (2, 1, 3)]

    def half_sum(both):
        return ((both[0].astype(F32) + both[1].astype(F32)) + (both[2].astype(F32) + both[3].astype(F32))).astype(BF)

    def window(both, half, h):
        return call(
            functools.partial(window_kernel, h),
            (jax.ShapeDtypeStruct((2, ROWS, NS), BF), jax.ShapeDtypeStruct((PC, NT, NS), BF)),
            f"window{h}",
            cost_estimate=cost(2),
        )(*both, half, onset_source, t_samp, t_spec)

    sum_a = summed(*convolve(pieces, held, 0))
    both_a = over_y(sum_a)
    sum_b = summed(*convolve(pieces, held, 1))
    both_a[1:], sum_b = together(both_a[1:], sum_b)
    both_b = over_y(sum_b)
    half_a = send(half_sum(both_a), "rcv", to_zh)
    half_b = send(half_sum(both_b), "rcv", to_zh)
    [half_a], both_b = together([half_a], both_b)
    wave_a, field_a = window(both_a, half_a, 0)
    wave_b, field_b = window(both_b, half_b, 1)
    own_a = over_y([wave_a] * 4)
    own_b = over_y([wave_b] * 4)
    upgoing = call(
        flip_kernel, jax.ShapeDtypeStruct((NP, NS, NT), BF), "flip", cost_estimate=cost(2)
    )(field_a, field_b)
    parts = []
    own_a[:1], [upgoing] = together(own_a[:1], [upgoing])

    def over_core(own):
        return [*own, *[send(w, "rcv", to_core) for w in own]]

    def over_x(back):
        return [back[0]] + [send(back[d], "src", to_x(d)) for d in (2, 1, 3)]

    parts_a = over_x(correlate(over_core(own_a), held))
    own_b[2:], parts_a[:1] = together(own_b[2:], parts_a[:1])
    own_b[1:2], parts_a[2:3] = together(own_b[1:2], parts_a[2:3])
    parts = parts_a + over_x(correlate(over_core(own_b), held))

    keep, *gives = call(
        sum_kernel,
        [jax.ShapeDtypeStruct((CH, ROWS, NR), F32)] + [jax.ShapeDtypeStruct((CH, ROWS, NR), BF)] * 3,
        "sum_x",
    )(*parts)
    last = [send(gives[d - 1], "src", to_zl(d)) for d in (3, 2, 1)]
    refocused = call(
        refocus_kernel,
        jax.ShapeDtypeStruct((NP, NR, NT), F32),
        "refocus",
        in_specs=[pl.BlockSpec(memory_space=pltpu.VMEM)] * 7,
        out_specs=pl.BlockSpec(memory_space=pltpu.HBM),
        scratch_shapes=[pltpu.VMEM((NP, NR, NT), F32), pltpu.SemaphoreType.DMA((NP,))],
    )(
        *last, keep, direct, onset_receiver.T, t_samp
    )
    return (upgoing, refocused)


def solution(mesh):
    in_specs = (
        P(None, None, "src", "rcv"),
        P("src", "rcv", None),
        P("src", "rcv", None),
        P(None, "src"),
        P("src", "rcv"),
    )
    out_specs = (P("rcv", "src", None), P("src", "rcv", None))
    return jax.shard_map(
        on_device, mesh=mesh, in_specs=in_specs, out_specs=out_specs, check_vma=False
    )
```
